256 devices in a mesh: row: 16 (over y, x), col: 16 (over z, core).
Axes of the slice: x: 4, y: 4, z: 8, core: 2. Of those that a mesh axis runs over, the one named last changes fastest.
Arguments:
- panel: bfloat16 [15, 32, 512, 512], P(None, 'row', 'col'), may hold values from -0.109375 to 0.109375
- diag_inverse: float32 [6, 32, 512, 512], P(None, 'row', 'col'), as said below
- parents: int32 [5, 32], replicated, may hold values from 0 to 31, as said below
- supernode_sizes: int32 [6, 32], replicated, may hold values from 128 to 512
Outputs:
- cross: float32 [15, 32, 512, 512], P(None, 'row', 'col')
- marginal: float32 [6, 32, 512, 512], P(None, 'row', 'col')
The draws below stay inside these ranges and needn't reach their ends.
Inputs may be any that keep to these rules, and one draw needn't show every extreme that they name: `parents`: the parent of a supernode g of level d + 1 is a supernode of level d whose index divided by 2 equals g divided by 2, or that minus 1 modulo 32 / 2. `diag_inverse`: every block is symmetric and positive definite.
All inputs are finite; a program needn't handle non-finite values.
Results may differ from the reference program's by a relative error of at most 0.0023.
Values may be sent and summed in bfloat16 or wider, within the bound.
A program may use at most 128 MiB of HBM per device.

```python
import jax
import jax.numpy as jnp
from jax import lax

W = 512
LEVELS = 6
NPR = 2
NODES = 32
PAIRS = 15


def draw_diag_inverse(key, part):
    first = jax.random.fold_in(jax.random.fold_in(key, 11), 0)
    basis = jax.random.normal(first, (LEVELS, NODES, W, W), jnp.float32)
    gram = jnp.einsum('abij,abkj->abik', basis, basis, precision=lax.Precision.HIGHEST) / (2.0 * W)
    gram = 0.5 * (gram + jnp.swapaxes(gram, 2, 3)) + 0.5 * jnp.eye(W, dtype=jnp.float32)[None, None]
    return gram


def draw_parents(key, part):
    first, second, third = jax.random.split(jax.random.fold_in(key, 23), 3)
    indices = jnp.arange(NODES, dtype=jnp.int32)
    row_count = NODES // NPR
    own_rows = indices // NPR
    side = jax.random.randint(first, (LEVELS - 1, NODES), 0, 2, jnp.int32)
    within = jnp.minimum(jax.random.randint(second, (LEVELS - 1, NODES), 0, NPR, jnp.int32), jax.random.randint(third, (LEVELS - 1, NODES), 0, NPR, jnp.int32))
    source_rows = (own_rows[None, :] - side + row_count) % row_count
    return (source_rows * NPR + within).astype(jnp.int32)


def plant(entries, stream_key, low, top_value):
    longest = entries.shape.index(max(entries.shape))
    spots = []
    for shift in (0, 1):
        where = [jax.random.randint(jax.random.fold_in(stream_key, axis), (), 0, length) for axis, length in enumerate(entries.shape)]
        where[longest] = (where[longest] + shift) % entries.shape[longest]
        spots.append(tuple(where))
    return entries.at[spots[0]].set(low).at[spots[1]].set(top_value)


def levels(stream_key, extent, cuts, least, largest):
    def one(position, shards_of):
        steps = jax.random.uniform(jax.random.fold_in(jax.random.fold_in(stream_key, 6), position), (shards_of,), jnp.float32, least / len(cuts), largest / len(cuts))
        return jnp.repeat(jnp.exp(steps), extent[position] // shards_of).reshape((-1,) + (1,) * (len(extent) - position - 1))

    loudness = one(*cuts[0])
    for cut in cuts[1:]:
        loudness = loudness * one(*cut)
    return loudness


def scatter_about(stream_key, dims, width, most, shards=(), kind=jnp.bfloat16):
    drawn = jax.random.normal(stream_key, dims, jnp.float32) * width
    if len(shards) > 0:
        drawn = levels(stream_key, dims, shards, -0.22, 0.18) * drawn
    return jnp.clip(drawn, min=-most, max=most).astype(kind)


def setup_inputs(seed: int = 0) -> dict:
    seeds = jax.random.split(jax.random.key(seed), 5)
    panel = scatter_about(seeds[0], (PAIRS, NODES, W, W), (W * LEVELS) ** -0.5, 0.109375, ((1, 16), (2, 16)))
    diag_inverse = draw_diag_inverse(jax.random.fold_in(seeds[4], 71), 0)
    parents = draw_parents(jax.random.fold_in(seeds[4], 71), 0)
    supernode_sizes = plant(jax.random.randint(seeds[3], (LEVELS, NODES), W // 4, W + 1), jax.random.fold_in(seeds[3], 1), W // 4, W).astype(jnp.int32)
    return dict(panel=panel, diag_inverse=diag_inverse, parents=parents, supernode_sizes=supernode_sizes)


def reference(panel, diag_inverse, parents, supernode_sizes):
    columns = jnp.arange(W, dtype=jnp.int32)
    identity = jnp.eye(W, dtype=jnp.float32)
    ancestry_ids = jnp.zeros((0, NODES), jnp.int32)
    crosses = []
    diagonals = []
    chain = None
    for level in range(LEVELS):
        live_cols = (columns[None, :] < supernode_sizes[level][:, None]).astype(jnp.float32)
        diag_base = diag_inverse[level] * live_cols[:, :, None] * live_cols[:, None, :] + identity[None] * (1.0 - live_cols)[:, None, :]
        if level == 0:
            diagonal = diag_base
        else:
            parent_ids = parents[level - 1].astype(jnp.int32)
            ancestry_ids = jnp.concatenate([ancestry_ids[:, parent_ids], parent_ids[None, :]], axis=0)
            upper_sizes = supernode_sizes[jnp.arange(level, dtype=jnp.int32)[:, None], ancestry_ids]
            live_upper = (columns[None, None, :] < upper_sizes[:, :, None]).astype(jnp.float32)
            start = level * (level - 1) // 2
            block = panel[start:start + level].astype(jnp.float32) * live_upper[:, :, :, None] * live_cols[None, :, None, :]
            lower = jnp.transpose(block, (1, 0, 2, 3))
            ancestry = chain[parent_ids]
            cross = -jnp.einsum("nlmik,nmkj->nlij", ancestry, lower, precision=lax.Precision.HIGHEST)
            diagonal = diag_base - jnp.einsum("nlki,nlkj->nij", lower, cross, precision=lax.Precision.HIGHEST)
            crosses.append(jnp.transpose(cross, (1, 0, 2, 3)))
        diagonals.append(diagonal)
        if level < LEVELS - 1:
            if level == 0:
                chain = diagonal[:, None, None]
            else:
                upper = jnp.concatenate([ancestry, cross[:, :, None]], axis=2)
                bottom = jnp.concatenate([jnp.swapaxes(cross, 2, 3)[:, None], diagonal[:, None, None]], axis=2)
                chain = jnp.concatenate([upper, bottom], axis=1)
    return jnp.concatenate(crosses, axis=0), jnp.stack(diagonals)
```

```python
import functools

import jax
import jax.numpy as jnp
from jax import lax
from jax.experimental import pallas as pl
from jax.experimental.pallas import tpu as pltpu
from jax.sharding import PartitionSpec as P

MESH = pl.DeviceIdType.MESH
LEVELS = 6
F32 = jnp.float32
BF16 = jnp.bfloat16


def lanes_of(level):
    return 128 * (-(-32 * level // 128))


def kernel(rows_n, cols_n, panel, diag, parents, sizes, cross_out, marg_out, *scratch):
    cands = scratch[0:5]
    fulls = scratch[5:10]
    turn_out = scratch[10:15]
    turn_in = scratch[15:20]
    lhs, acc, ring_send, ring_recv, mate_send, mate_recv, chain_send, chain_recv, turn_send, turn_recv = scratch[20:]
    width = diag.shape[3]
    lines = diag.shape[2]
    chips = cols_n // 2
    row = lax.axis_index("row")
    col = lax.axis_index("col")
    chip = col // 2
    core = col % 2
    mate = col + 1 - 2 * core
    right = (col + 2) % cols_n
    left = (col + cols_n - 2) % cols_n
    next_row = (row + 1) % rows_n
    prev_row = (row + rows_n - 1) % rows_n

    barrier = pltpu.get_barrier_semaphore()
    for k in range(1, cols_n):
        pl.semaphore_signal(barrier, inc=1, device_id=(row, (col + k) % cols_n), device_id_type=MESH)
    pl.semaphore_signal(barrier, inc=1, device_id=(next_row, col), device_id_type=MESH)
    pl.semaphore_signal(barrier, inc=1, device_id=(prev_row, col), device_id_type=MESH)
    pl.semaphore_wait(barrier, cols_n + 1)

    line_of = lax.broadcasted_iota(jnp.int32, (lines, width), 0) + col * lines
    column_of = lax.broadcasted_iota(jnp.int32, (lines, width), 1)

    def base_of(level, n):
        size = sizes[level, row * 2 + n]
        live = (line_of < size) & (column_of < size)
        eye = (line_of == column_of) & (line_of >= size)
        return jnp.where(live, diag[level, n], jnp.where(eye, 1.0, 0.0))

    def strip(level, at, first, count):
        return fulls[level - 1].at[
            pl.ds(first, count), pl.ds(pl.multiple_of(at * lines, lines), lines), :
        ]

    def share(level, way, step):
        if step < 3:
            return 0, 2 * level
        return (0, level) if way == 0 else (level, level)

    def ring_copy(level, way, step, arriving):
        hop = step + 1 if arriving else step
        at = ((chip - hop + chips) % chips if way == 0 else (chip + hop) % chips) * 2 + core
        piece = strip(level, at, *share(level, way, step))
        return pltpu.make_async_remote_copy(
            src_ref=piece, dst_ref=piece,
            send_sem=ring_send.at[level - 1, way, step],
            recv_sem=ring_recv.at[level - 1, way, step],
            device_id=(row, right if way == 0 else left), device_id_type=MESH,
        )

    def mate_copy(level, index, arriving):
        whose = 1 - core if arriving else core
        if index == 0:
            at, part = chip, (0, 2 * level)
        else:
            way, step = (index - 1) // 4, (index - 1) % 4
            at = (chip - step - 1 + chips) % chips if way == 0 else (chip + step + 1) % chips
            part = share(level, way, step)
        piece = strip(level, at * 2 + whose, *part)
        return pltpu.make_async_remote_copy(
            src_ref=piece, dst_ref=piece,
            send_sem=mate_send.at[level - 1, index],
            recv_sem=mate_recv.at[level - 1, index],
            device_id=(row, mate), device_id_type=MESH,
        )

    def mask_factor(level):
        start = level * (level - 1) // 2

        def one(n, _):
            node = row * 2 + n
            size = sizes[level, node]
            above = node
            for up in range(level - 1, -1, -1):
                above = parents[up, above]
                upper = sizes[up, above]
                keep = (line_of < upper) & (column_of < size)
                block = jnp.where(keep, panel[start + up, n].astype(F32), 0.0)
                fulls[level - 1][
                    n * level + up, pl.ds(pl.multiple_of(col * lines, lines), lines), :
                ] = block.astype(BF16)
            return 0

        lax.fori_loop(0, 2, one, 0)

    def ring(level, step):
        for way in (0, 1):
            if step > 0:
                ring_copy(level, way, step - 1, True).wait_recv()
            if step < 4:
                ring_copy(level, way, step, False).start()
        if step == 0:
            mate_copy(level, 0, False).start()
        else:
            mate_copy(level, step, False).start()
            mate_copy(level, 4 + step, False).start()

    def ring_end(level):
        for index in range(9):
            mate_copy(level, index, True).wait_recv()

    def chain_part(level, n, part, there):
        d = level
        first, count = ((0, d * d), (d * d, d), (d * d + d, d), (d * d + 2 * d, 1))[part]
        return cands[d].at[n + 2 if there else n, pl.ds(first, count)]

    def chain_copy(level, n, part):
        return pltpu.make_async_remote_copy(
            src_ref=chain_part(level, n, part, False),
            dst_ref=chain_part(level, n, part, True),
            send_sem=chain_send.at[level, n, part],
            recv_sem=chain_recv.at[level, n, part],
            device_id=(next_row, col), device_id_type=MESH,
        )

    def turn_copy(level, n, k):
        there = (col + k) % cols_n
        return pltpu.make_async_remote_copy(
            src_ref=turn_out[level - 1].at[n, there],
            dst_ref=turn_in[level - 1].at[n, col],
            send_sem=turn_send.at[level - 1, n, k],
            recv_sem=turn_recv.at[level - 1, n, k],
            device_id=(row, there), device_id_type=MESH,
        )

    def turn_arrival(level, n, k):
        whence = (col + cols_n - k) % cols_n
        return pltpu.make_async_remote_copy(
            src_ref=turn_out[level - 1].at[n, whence],
            dst_ref=turn_in[level - 1].at[n, whence],
            send_sem=turn_send.at[level - 1, n, k],
            recv_sem=turn_recv.at[level - 1, n, k],
            device_id=(row, whence), device_id_type=MESH,
        )

    def parts_of(level):
        return (3,) if level == 0 else (0, 1, 2, 3)

    def split(value):
        high = value.astype(BF16)
        return high, (value - high.astype(F32)).astype(BF16)

    def select_and_cross(level):
        d = level - 1
        start = level * (level - 1) // 2
        tall = lines * level

        def one(n, _):
            node = row * 2 + n
            parent = parents[d, node]
            own = (parent >= row * 2) & (parent < row * 2 + 2)
            slot = jnp.where(own, 0, 2) + lax.rem(parent, 2)
            for l in range(level):
                for m in range(level):
                    if l < d and m < d:
                        entry = l * d + m
                    elif l < d:
                        entry = d * d + l
                    elif m < d:
                        entry = d * d + d + m
                    else:
                        entry = d * d + 2 * d
                    value = cands[d][slot, entry]
                    if level < LEVELS - 1:
                        cands[level][n, l * level + m] = value
                    high, low = split(value)
                    lhs[m, l * lines : (l + 1) * lines, :] = high
                    lhs[m, tall + l * lines : tall + (l + 1) * lines, :] = low
            if level < LEVELS - 1:
                chain_copy(level, n, 0).start()
            acc[0 : 2 * tall, :] = jnp.zeros((2 * tall, width), F32)

            def add(m, _):
                acc[0 : 2 * tall, :] += jnp.dot(
                    lhs[m, 0 : 2 * tall, :], fulls[level - 1][n * level + m], preferred_element_type=F32
                )
                return 0

            lax.fori_loop(0, level, add, 0)
            crossed = -(acc[0:tall, :] + acc[tall : 2 * tall, :])
            for l in range(level):
                piece = crossed[l * lines : (l + 1) * lines, :]
                cross_out[start + l, n] = piece
                if level < LEVELS - 1:
                    cands[level][n, level * level + l] = piece
            if level < LEVELS - 1:
                chain_copy(level, n, 1).start()
            turned = jnp.transpose(crossed, (1, 0))
            for c in range(cols_n):
                turn_out[level - 1][n, c, :, 0:tall] = turned[c * lines : (c + 1) * lines, :]

            def send(k, _):
                turn_copy(level, n, k).start()
                return 0

            lax.fori_loop(1, cols_n, send, 0)
            turn_in[level - 1][n, col] = turn_out[level - 1][n, col]
            return 0

        lax.fori_loop(0, 2, one, 0)

    lane_of = lax.broadcasted_iota(jnp.int32, (lines, 128), 1)
    per = 128 // lines

    def finish_level(level):
        def one(n, _):
            def arrive(k, _):
                turn_arrival(level, n, k).wait_recv()
                return 0

            lax.fori_loop(1, cols_n, arrive, 0)
            for l in range(level):
                for q in range(width // 128):
                    piece = None
                    for k in range(per):
                        source = turn_in[level - 1][
                            n, q * per + k, :, (l // per) * 128 : (l // per) * 128 + 128
                        ]
                        shift = ((k - l % per) * lines) % 128
                        if shift:
                            source = pltpu.roll(source, shift, 1)
                        piece = source if piece is None else jnp.where(lane_of >= k * lines, source, piece)
                    high, low = split(piece)
                    lhs[l, 0:lines, q * 128 : (q + 1) * 128] = high
                    lhs[l, lines : 2 * lines, q * 128 : (q + 1) * 128] = low
                    if level < LEVELS - 1:
                        cands[level][n, level * level + level + l, :, q * 128 : (q + 1) * 128] = piece
            if level < LEVELS - 1:
                chain_copy(level, n, 2).start()
            acc[0 : 2 * lines, :] = jnp.zeros((2 * lines, width), F32)

            def add(l, _):
                acc[0 : 2 * lines, :] += jnp.dot(
                    lhs[l, 0 : 2 * lines, :], fulls[level - 1][n * level + l], preferred_element_type=F32
                )
                return 0

            lax.fori_loop(0, level, add, 0)
            marginal = base_of(level, n) - (acc[0:lines, :] + acc[lines : 2 * lines, :])
            marg_out[level, n] = marginal
            if level < LEVELS - 1:
                cands[level][n, level * level + 2 * level] = marginal
                chain_copy(level, n, 3).start()
            return 0

        lax.fori_loop(0, 2, one, 0)

    mask_factor(1)
    ring(1, 0)
    for n in range(2):
        marginal = base_of(0, n)
        marg_out[0, n] = marginal
        cands[0][n, 0] = marginal
        chain_copy(0, n, 3).start()
    mask_factor(2)
    ring(2, 0)
    ring(1, 1)
    mask_factor(3)
    ring(2, 1)
    ring(1, 2)
    mask_factor(4)
    ring(2, 2)
    ring(1, 3)
    mask_factor(5)
    ring(2, 3)
    ring(3, 0)
    ring(1, 4)
    before = {1: (), 2: ((2, 4),), 3: ((3, 4),), 4: ((4, 4),), 5: ((5, 4),)}
    middle = {1: ((3, 1), (3, 2)), 2: ((4, 0), (4, 1)), 3: ((5, 1), (5, 2)), 4: (), 5: ()}
    after = {1: ((3, 3),), 2: ((4, 2), (4, 3), (5, 0)), 3: ((5, 3),), 4: (), 5: ()}
    for level in range(1, LEVELS):
        for job in before[level]:
            ring(*job)
        ring_end(level)
        for n in range(2):
            for part in parts_of(level - 1):
                chain_copy(level - 1, n, part).wait_recv()
        select_and_cross(level)
        for job in middle[level]:
            ring(*job)
        finish_level(level)
        for job in after[level]:
            ring(*job)

    for level in range(1, LEVELS):
        for way in (0, 1):
            for step in range(4):
                ring_copy(level, way, step, False).wait_send()
        for index in range(9):
            mate_copy(level, index, False).wait_send()

        def sent(k, _):
            turn_copy(level, 0, k).wait_send()
            turn_copy(level, 1, k).wait_send()
            return 0

        lax.fori_loop(1, cols_n, sent, 0)
    for level in range(LEVELS - 1):
        for n in range(2):
            for part in parts_of(level):
                chain_copy(level, n, part).wait_send()


def solution(mesh):
    rows_n, cols_n = mesh.shape["row"], mesh.shape["col"]

    def shards(panel, diag_inverse, parents, sizes):
        pairs, per, lines, width = panel.shape
        vmem = pl.BlockSpec(memory_space=pltpu.VMEM)
        smem = pl.BlockSpec(memory_space=pltpu.SMEM)
        dma = pltpu.SemaphoreType.DMA
        return pl.pallas_call(
            functools.partial(kernel, rows_n, cols_n),
            out_shape=(
                jax.ShapeDtypeStruct((pairs, per, lines, width), F32),
                jax.ShapeDtypeStruct((LEVELS, per, lines, width), F32),
            ),
            in_specs=[vmem, vmem, smem, smem],
            out_specs=(vmem, vmem),
            scratch_shapes=[
                *[pltpu.VMEM((4, (d + 1) * (d + 1), lines, width), F32) for d in range(5)],
                *[pltpu.VMEM((2 * d, width, width), BF16) for d in range(1, 6)],
                *[pltpu.VMEM((2, cols_n, lines, lanes_of(d)), F32) for d in range(1, 6)],
                *[pltpu.VMEM((2, cols_n, lines, lanes_of(d)), F32) for d in range(1, 6)],
                pltpu.VMEM((5, 320, width), BF16),
                pltpu.VMEM((320, width), F32),
                dma((5, 2, 4)),
                dma((5, 2, 4)),
                dma((5, 9)),
                dma((5, 9)),
                dma((5, 2, 4)),
                dma((5, 2, 4)),
                dma((5, 2, cols_n)),
                dma((5, 2, cols_n)),
            ],
            compiler_params=pltpu.CompilerParams(
                collective_id=0, has_side_effects=True, vmem_limit_bytes=64000 * 1024
            ),
        )(panel, diag_inverse, parents, sizes)

    in_specs = (P(None, "row", "col", None), P(None, "row", "col", None), P(), P())
    out_specs = (P(None, "row", "col", None), P(None, "row", "col", None))
    return jax.shard_map(shards, mesh=mesh, in_specs=in_specs, out_specs=out_specs, check_vma=False)
```

```python
import functools

import jax
import jax.numpy as jnp
from jax import lax
from jax.experimental import pallas as pl
from jax.experimental.pallas import tpu as pltpu
from jax.sharding import PartitionSpec as P

MESH = pl.DeviceIdType.MESH
LEVELS = 6
F32 = jnp.float32
BF16 = jnp.bfloat16


POWER = 6


def joint(level):
    return level <= 2


def lanes_of(level):
    tall = 32 * level * (2 if joint(level) else 1)
    return 128 * (-(-tall // 128))


def scale_of(value):
    top = jnp.max(jnp.max(jnp.abs(value), axis=0, keepdims=True), axis=1, keepdims=True)
    return jnp.maximum(top, 1e-30).astype(BF16).astype(F32)


def encode(value, scale):
    unit = value * (1.0 / scale)
    square = unit * unit
    return unit * jnp.abs(unit) * (square * square)


def decode(code):
    root = jnp.exp(jnp.log(jnp.abs(code)) * (1.0 / POWER))
    return jnp.where(code > 0.0, root, jnp.where(code < 0.0, -root, 0.0))


def kernel(rows_n, cols_n, panel, diag, parents, sizes, cross_out, marg_out, *scratch):
    cands = scratch[0:5]
    fulls = scratch[5:10]
    turn_out = scratch[10:15]
    turn_in = scratch[15:20]
    scales = scratch[20:25]
    (
        lhs, acc, opened, turned_f32, ring_send, ring_recv, mate_send, mate_recv,
        chain_send, chain_recv, scale_send, scale_recv, turn_send, turn_recv,
    ) = scratch[25:]
    width = diag.shape[3]
    lines = diag.shape[2]
    chips = cols_n // 2
    row = lax.axis_index("row")
    col = lax.axis_index("col")
    chip = col // 2
    core = col % 2
    mate = col + 1 - 2 * core
    right = (col + 2) % cols_n
    left = (col + cols_n - 2) % cols_n
    next_row = (row + 1) % rows_n
    prev_row = (row + rows_n - 1) % rows_n

    barrier = pltpu.get_barrier_semaphore()
    for k in range(1, cols_n):
        pl.semaphore_signal(barrier, inc=1, device_id=(row, (col + k) % cols_n), device_id_type=MESH)
    pl.semaphore_signal(barrier, inc=1, device_id=(next_row, col), device_id_type=MESH)
    pl.semaphore_signal(barrier, inc=1, device_id=(prev_row, col), device_id_type=MESH)
    pl.semaphore_wait(barrier, cols_n + 1)

    line_of = lax.broadcasted_iota(jnp.int32, (lines, width), 0) + col * lines
    column_of = lax.broadcasted_iota(jnp.int32, (lines, width), 1)

    def base_of(level, n):
        size = sizes[level, row * 2 + n]
        live = (line_of < size) & (column_of < size)
        eye = (line_of == column_of) & (line_of >= size)
        return jnp.where(live, diag[level, n], jnp.where(eye, 1.0, 0.0))

    def strip(level, at, first, count):
        return fulls[level - 1].at[
            pl.ds(first, count), pl.ds(pl.multiple_of(at * lines, lines), lines), :
        ]

    def goes(n, way, step):
        return step < 3 or (step == 3 and way == n)

    def ring_copy(level, n, way, step, arriving):
        hop = step + 1 if arriving else step
        at = ((chip - hop + chips) % chips if way == 0 else (chip + hop) % chips) * 2 + core
        piece = strip(level, at, n * level, level)
        return pltpu.make_async_remote_copy(
            src_ref=piece, dst_ref=piece,
            send_sem=ring_send.at[level - 1, n, way, step],
            recv_sem=ring_recv.at[level - 1, n, way, step],
            device_id=(row, right if way == 0 else left), device_id_type=MESH,
        )

    def mate_copy(level, n, way, step, arriving):
        whose = 1 - core if arriving else core
        if step < 0:
            at, index = chip, 0
        else:
            at = (chip - step - 1 + chips) % chips if way == 0 else (chip + step + 1) % chips
            index = 1 + way * 4 + step
        piece = strip(level, at * 2 + whose, n * level, level)
        return pltpu.make_async_remote_copy(
            src_ref=piece, dst_ref=piece,
            send_sem=mate_send.at[level - 1, n, index],
            recv_sem=mate_recv.at[level - 1, n, index],
            device_id=(row, mate), device_id_type=MESH,
        )

    def mask_factor(level):
        start = level * (level - 1) // 2

        def one(n, _):
            node = row * 2 + n
            size = sizes[level, node]
            above = node
            for up in range(level - 1, -1, -1):
                above = parents[up, above]
                upper = sizes[up, above]
                keep = (line_of < upper) & (column_of < size)
                block = jnp.where(keep, panel[start + up, n].astype(F32), 0.0)
                fulls[level - 1][
                    n * level + up, pl.ds(pl.multiple_of(col * lines, lines), lines), :
                ] = block.astype(BF16)
            return 0

        lax.fori_loop(0, 2, one, 0)

    def ring(level, step):
        for n in (0, 1):
            for way in (0, 1):
                if step > 0 and goes(n, way, step - 1):
                    ring_copy(level, n, way, step - 1, True).wait_recv()
                if goes(n, way, step):
                    ring_copy(level, n, way, step, False).start()
            for way in (0, 1):
                if step == 0 and way == 0:
                    mate_copy(level, n, 0, -1, False).start()
                if step > 0 and goes(n, way, step - 1):
                    mate_copy(level, n, way, step - 1, False).start()

    def mates(n):
        yield 0, -1
        for way in (0, 1):
            for step in range(4):
                if goes(n, way, step):
                    yield way, step

    def ring_end(level):
        for n in (0, 1):
            for way, step in mates(n):
                mate_copy(level, n, way, step, True).wait_recv()

    def chain_part(level, n, part, there):
        d = level
        first, count = ((0, d * d), (d * d, d), (d * d + d, d), (d * d + 2 * d, 1))[part]
        return cands[d].at[n + 2 if there else n, pl.ds(first, count)]

    def chain_copy(level, n, part):
        return pltpu.make_async_remote_copy(
            src_ref=chain_part(level, n, part, False),
            dst_ref=chain_part(level, n, part, True),
            send_sem=chain_send.at[level, n, part],
            recv_sem=chain_recv.at[level, n, part],
            device_id=(next_row, col), device_id_type=MESH,
        )

    def scale_copy(level, n, part):
        rows = pl.ds(0, 16 if part == 0 else 8)
        return pltpu.make_async_remote_copy(
            src_ref=scales[level].at[n, part, rows],
            dst_ref=scales[level].at[n + 2, part, rows],
            send_sem=scale_send.at[level, n, part],
            recv_sem=scale_recv.at[level, n, part],
            device_id=(next_row, col), device_id_type=MESH,
        )

    def pass_on(level, n, part):
        scale_copy(level, n, part).start()
        chain_copy(level, n, part).start()

    def turn_copy(level, n, k):
        there = (col + k) % cols_n
        return pltpu.make_async_remote_copy(
            src_ref=turn_out[level - 1].at[n, there],
            dst_ref=turn_in[level - 1].at[n, col],
            send_sem=turn_send.at[level - 1, n, k],
            recv_sem=turn_recv.at[level - 1, n, k],
            device_id=(row, there), device_id_type=MESH,
        )

    def turn_arrival(level, n, k):
        whence = (col + cols_n - k) % cols_n
        return pltpu.make_async_remote_copy(
            src_ref=turn_out[level - 1].at[n, whence],
            dst_ref=turn_in[level - 1].at[n, whence],
            send_sem=turn_send.at[level - 1, n, k],
            recv_sem=turn_recv.at[level - 1, n, k],
            device_id=(row, whence), device_id_type=MESH,
        )

    def parts_of(level):
        return (3,) if level == 0 else (0, 1, 2, 3)

    def split(value):
        high = value.astype(BF16)
        return high, (value - high.astype(F32)).astype(BF16)

    lane_of = lax.broadcasted_iota(jnp.int32, (lines, 128), 1)
    per = 128 // lines
    sixteenth = lax.broadcasted_iota(jnp.int32, (16, 128), 0)

    def wide(scale):
        return jnp.concatenate([scale] * (width // 128), axis=1)

    def select_and_cross(level):
        d = level - 1
        start = level * (level - 1) // 2
        tall = lines * level

        def one(n, _):
            node = row * 2 + n
            parent = parents[d, node]
            own = (parent >= row * 2) & (parent < row * 2 + 2)
            slot = jnp.where(own, 0, 2) + lax.rem(parent, 2)
            old = scales[d][slot, 0] if d else None
            fresh = [scales[d][slot, part, 0:8, :] if d or part == 3 else None for part in (1, 2, 3)]
            for l in range(level):
                for m in range(level):
                    if l < d and m < d:
                        entry = l * d + m
                        which = 3 * max(l, m) + (2 if l == m else 0 if l < m else 1)
                        scale = old[which : which + 1, :]
                    elif l < d:
                        entry, scale = d * d + l, fresh[0][0:1, :]
                    elif m < d:
                        entry, scale = d * d + d + m, fresh[1][0:1, :]
                    else:
                        entry, scale = d * d + 2 * d, fresh[2][0:1, :]
                    code = cands[d][slot, entry]
                    if level < LEVELS - 1:
                        cands[level][n, l * level + m] = code
                    high, low = split(decode(code.astype(F32)) * wide(scale))
                    lhs[m, l * lines : (l + 1) * lines, :] = high
                    lhs[m, tall + l * lines : tall + (l + 1) * lines, :] = low
            if level < LEVELS - 1:
                table = old
                for part in (0, 1, 2):
                    if fresh[part] is not None:
                        line = jnp.broadcast_to(fresh[part][0:1, :], (16, 128))
                        table = line if table is None else jnp.where(sixteenth == 3 * d + part, line, table)
                scales[level][n, 0] = table
                pass_on(level, n, 0)
            acc[0 : 2 * tall, :] = jnp.zeros((2 * tall, width), F32)

            def add(m, _):
                acc[0 : 2 * tall, :] += jnp.dot(
                    lhs[m, 0 : 2 * tall, :], fulls[level - 1][n * level + m], preferred_element_type=F32
                )
                return 0

            lax.fori_loop(0, level, add, 0)
            crossed = -(acc[0:tall, :] + acc[tall : 2 * tall, :])
            scale = scale_of(crossed)
            code = encode(crossed, scale)
            for l in range(level):
                cross_out[start + l, n] = crossed[l * lines : (l + 1) * lines, :]
                if level < LEVELS - 1:
                    cands[level][n, level * level + l] = code[l * lines : (l + 1) * lines, :].astype(BF16)
            if level < LEVELS - 1:
                scales[level][n, 1, 0:8, :] = jnp.broadcast_to(scale, (8, 128))
                pass_on(level, n, 1)
            turned = jnp.transpose(code, (1, 0)).astype(BF16)
            slab = 0 if joint(level) else n
            first = n * tall if joint(level) else 0
            for c in range(cols_n):
                turn_out[level - 1][slab, c, 0:lines, first : first + tall] = turned[
                    c * lines : (c + 1) * lines, :
                ]
                turn_out[level - 1][slab, c, lines : lines + 16, first : first + tall] = (
                    jnp.broadcast_to(scale, (16, tall)).astype(BF16)
                )
            if not joint(level):
                send_turn(level, n)
            return 0

        if joint(level):
            one(0, 0)
            one(1, 0)
            send_turn(level, 0)
        else:
            lax.fori_loop(0, 2, one, 0)

    def send_turn(level, slab):
        def send(k, _):
            turn_copy(level, slab, k).start()
            return 0

        lax.fori_loop(1, cols_n, send, 0)
        turn_in[level - 1][slab, col] = turn_out[level - 1][slab, col]

    def open_turn(level, slab):
        def arrive(k, _):
            turn_arrival(level, slab, k).wait_recv()
            return 0

        lax.fori_loop(1, cols_n, arrive, 0)

        lanes = lanes_of(level)

        def undo(c, _):
            code = turn_in[level - 1][slab, c, 0:lines, :].astype(F32)
            scale = turn_in[level - 1][slab, c, lines : lines + 16, :].astype(F32)
            opened[c, :, 0:lanes] = decode(code) * jnp.concatenate([scale] * (lines // 16), axis=0)
            return 0

        lax.fori_loop(0, cols_n, undo, 0)

    def finish_level(level):
        def one(n, _):
            if not joint(level):
                open_turn(level, n)
            for l in range(level):
                group = l + n * level if joint(level) else l
                for q in range(width // 128):
                    piece = None
                    for k in range(per):
                        source = opened[
                            q * per + k, :, (group // per) * 128 : (group // per) * 128 + 128
                        ]
                        shift = ((k - group % per) * lines) % 128
                        if shift:
                            source = pltpu.roll(source, shift, 1)
                        piece = source if piece is None else jnp.where(lane_of >= k * lines, source, piece)
                    high, low = split(piece)
                    lhs[l, 0:lines, q * 128 : (q + 1) * 128] = high
                    lhs[l, lines : 2 * lines, q * 128 : (q + 1) * 128] = low
                    if level < LEVELS - 1:
                        turned_f32[l * lines : (l + 1) * lines, q * 128 : (q + 1) * 128] = piece
            if level < LEVELS - 1:
                whole = turned_f32[0 : level * lines, :]
                scale = scale_of(whole)
                code = encode(whole, scale).astype(BF16)
                for l in range(level):
                    cands[level][n, level * level + level + l] = code[l * lines : (l + 1) * lines, :]
                scales[level][n, 2, 0:8, :] = jnp.broadcast_to(scale, (8, 128))
                pass_on(level, n, 2)
            acc[0 : 2 * lines, :] = jnp.zeros((2 * lines, width), F32)

            def add(l, _):
                acc[0 : 2 * lines, :] += jnp.dot(
                    lhs[l, 0 : 2 * lines, :], fulls[level - 1][n * level + l], preferred_element_type=F32
                )
                return 0

            lax.fori_loop(0, level, add, 0)
            marginal = base_of(level, n) - (acc[0:lines, :] + acc[lines : 2 * lines, :])
            marg_out[level, n] = marginal
            if level < LEVELS - 1:
                send_marginal(level, n, marginal)
            return 0

        if joint(level):
            open_turn(level, 0)
            one(0, 0)
            one(1, 0)
        else:
            lax.fori_loop(0, 2, one, 0)

    def send_marginal(level, n, marginal):
        scale = scale_of(marginal)
        cands[level][n, level * level + 2 * level] = encode(marginal, scale).astype(BF16)
        scales[level][n, 3, 0:8, :] = jnp.broadcast_to(scale, (8, 128))
        pass_on(level, n, 3)

    mask_factor(1)
    ring(1, 0)
    for n in range(2):
        marginal = base_of(0, n)
        marg_out[0, n] = marginal
        send_marginal(0, n, marginal)
    mask_factor(2)
    ring(2, 0)
    ring(1, 1)
    mask_factor(3)
    ring(2, 1)
    ring(1, 2)
    mask_factor(4)
    ring(2, 2)
    ring(1, 3)
    mask_factor(5)
    ring(2, 3)
    ring(3, 0)
    ring(1, 4)
    before = {1: (), 2: ((3, 3), (4, 0)), 3: ((4, 2),), 4: ((4, 4), (5, 1)), 5: ((5, 4),)}
    middle = {1: ((2, 4), (3, 1)), 2: ((3, 4), (4, 1)), 3: ((4, 3), (5, 0)), 4: ((5, 2), (5, 3)), 5: ()}
    after = {1: ((3, 2),), 2: (), 3: (), 4: (), 5: ()}
    for level in range(1, LEVELS):
        for job in before[level]:
            ring(*job)
        ring_end(level)
        for n in range(2):
            for part in parts_of(level - 1):
                scale_copy(level - 1, n, part).wait_recv()
                chain_copy(level - 1, n, part).wait_recv()
        select_and_cross(level)
        for job in middle[level]:
            ring(*job)
        finish_level(level)
        for job in after[level]:
            ring(*job)

    for level in range(1, LEVELS):
        for n in (0, 1):
            for way in (0, 1):
                for step in range(4):
                    if goes(n, way, step):
                        ring_copy(level, n, way, step, False).wait_send()
            for way, step in mates(n):
                mate_copy(level, n, way, step, False).wait_send()

        def sent(k, _):
            turn_copy(level, 0, k).wait_send()
            if not joint(level):
                turn_copy(level, 1, k).wait_send()
            return 0

        lax.fori_loop(1, cols_n, sent, 0)
    for level in range(LEVELS - 1):
        for n in range(2):
            for part in parts_of(level):
                scale_copy(level, n, part).wait_send()
                chain_copy(level, n, part).wait_send()


def solution(mesh):
    rows_n, cols_n = mesh.shape["row"], mesh.shape["col"]

    def shards(panel, diag_inverse, parents, sizes):
        pairs, per, lines, width = panel.shape
        vmem = pl.BlockSpec(memory_space=pltpu.VMEM)
        smem = pl.BlockSpec(memory_space=pltpu.SMEM)
        dma = pltpu.SemaphoreType.DMA

        def turn_shape(level):
            return (1 if joint(level) else 2, cols_n, lines + 16, lanes_of(level))

        return pl.pallas_call(
            functools.partial(kernel, rows_n, cols_n),
            out_shape=(
                jax.ShapeDtypeStruct((pairs, per, lines, width), F32),
                jax.ShapeDtypeStruct((LEVELS, per, lines, width), F32),
            ),
            in_specs=[vmem, vmem, smem, smem],
            out_specs=(vmem, vmem),
            scratch_shapes=[
                *[pltpu.VMEM((4, (d + 1) * (d + 1), lines, width), BF16) for d in range(5)],
                *[pltpu.VMEM((2 * d, width, width), BF16) for d in range(1, 6)],
                *[pltpu.VMEM(turn_shape(d), BF16) for d in range(1, 6)],
                *[pltpu.VMEM(turn_shape(d), BF16) for d in range(1, 6)],
                *[pltpu.VMEM((4, 4, 16, 128), F32) for d in range(5)],
                pltpu.VMEM((5, 320, width), BF16),
                pltpu.VMEM((320, width), F32),
                pltpu.VMEM((cols_n, lines, 256), F32),
                pltpu.VMEM((4 * lines, width), F32),
                dma((5, 2, 2, 4)),
                dma((5, 2, 2, 4)),
                dma((5, 2, 9)),
                dma((5, 2, 9)),
                dma((5, 2, 4)),
                dma((5, 2, 4)),
                dma((5, 2, 4)),
                dma((5, 2, 4)),
                dma((5, 2, cols_n)),
                dma((5, 2, cols_n)),
            ],
            compiler_params=pltpu.CompilerParams(
                collective_id=0, has_side_effects=True, vmem_limit_bytes=64000 * 1024
            ),
        )(panel, diag_inverse, parents, sizes)

    in_specs = (P(None, "row", "col", None), P(None, "row", "col", None), P(), P())
    out_specs = (P(None, "row", "col", None), P(None, "row", "col", None))
    return jax.shard_map(shards, mesh=mesh, in_specs=in_specs, out_specs=out_specs, check_vma=False)
```

```python
import functools

import jax
import jax.numpy as jnp
from jax import lax
from jax.experimental import pallas as pl
from jax.experimental.pallas import tpu as pltpu
from jax.sharding import PartitionSpec as P

MESH = pl.DeviceIdType.MESH
LEVELS = 6
F32 = jnp.float32
BF16 = jnp.bfloat16


POWER = 6
PREPARE = ((2, 0), (1, 1), (2, 1), (1, 2), (2, 2), (1, 3), (2, 3), (3, 0), (1, 4))
BEFORE = {1: (), 2: ((3, 3), (4, 0)), 3: ((4, 2),), 4: ((4, 4), (5, 1)), 5: ((5, 4),)}
MIDDLE = {1: ((2, 4), (3, 1)), 2: ((3, 4), (4, 1)), 3: ((4, 3), (5, 0)), 4: ((5, 2), (5, 3)), 5: ()}
AFTER = {1: ((3, 2),), 2: (), 3: (), 4: (), 5: ()}


def joint(level):
    return level <= 2


def lanes_of(level):
    tall = 32 * level * (2 if joint(level) else 1)
    return 128 * (-(-tall // 128))


def scale_of(value):
    top = jnp.max(jnp.max(jnp.abs(value), axis=0, keepdims=True), axis=1, keepdims=True)
    return jnp.maximum(top, 1e-30).astype(BF16).astype(F32)


def encode(value, scale):
    unit = value * (1.0 / scale)
    square = unit * unit
    return unit * jnp.abs(unit) * (square * square)


def decode(code):
    root = jnp.exp(jnp.log(jnp.abs(code)) * (1.0 / POWER))
    return jnp.where(code > 0.0, root, jnp.where(code < 0.0, -root, 0.0))


def kernel(rows_n, cols_n, panel, diag, parents, sizes, cross_out, marg_out, *scratch):
    cands = scratch[0:5]
    fulls = scratch[5:10]
    turn_out = scratch[10:15]
    turn_in = scratch[15:20]
    scales = scratch[20:25]
    (
        lhs, acc, opened, turned_f32, mark_out, mark_in, factor_send, ring_recv, mate_recv,
        chain_send, chain_recv, scale_send, scale_recv, turn_send, turn_recv, mark_send, mark_recv,
    ) = scratch[25:]
    width = diag.shape[3]
    lines = diag.shape[2]
    chips = cols_n // 2
    row = lax.axis_index("row")
    col = lax.axis_index("col")
    chip = col // 2
    core = col % 2
    mate = col + 1 - 2 * core
    right = (col + 2) % cols_n
    left = (col + cols_n - 2) % cols_n
    next_row = (row + 1) % rows_n
    prev_row = (row + rows_n - 1) % rows_n

    barrier = pltpu.get_barrier_semaphore()
    for k in range(1, cols_n):
        pl.semaphore_signal(barrier, inc=1, device_id=(row, (col + k) % cols_n), device_id_type=MESH)
    pl.semaphore_signal(barrier, inc=1, device_id=(next_row, col), device_id_type=MESH)
    pl.semaphore_signal(barrier, inc=1, device_id=(prev_row, col), device_id_type=MESH)
    line_of = lax.broadcasted_iota(jnp.int32, (lines, width), 0) + col * lines
    column_of = lax.broadcasted_iota(jnp.int32, (lines, width), 1)

    def base_of(level, n):
        size = sizes[level, row * 2 + n]
        live = (line_of < size) & (column_of < size)
        eye = (line_of == column_of) & (line_of >= size)
        return jnp.where(live, diag[level, n], jnp.where(eye, 1.0, 0.0))

    def strip(level, at, first, count):
        return fulls[level - 1].at[
            pl.ds(first, count), pl.ds(pl.multiple_of(at * lines, lines), lines), :
        ]

    def goes(n, way, step):
        return step < 3 or (step == 3 and way == n)

    def ring_copy(level, n, way, step):
        at = ((chip - step + chips) % chips if way == 0 else (chip + step) % chips) * 2 + core
        piece = strip(level, at, n * level, level)
        return pltpu.make_async_remote_copy(
            src_ref=piece, dst_ref=piece,
            send_sem=factor_send.at[level - 1],
            recv_sem=ring_recv.at[level - 1, n, step],
            device_id=(row, right if way == 0 else left), device_id_type=MESH,
        )

    def mate_copy(level, n, way, step):
        if step < 0:
            at = chip
        else:
            at = (chip - step - 1 + chips) % chips if way == 0 else (chip + step + 1) % chips
        piece = strip(level, at * 2 + core, n * level, level)
        return pltpu.make_async_remote_copy(
            src_ref=piece, dst_ref=piece,
            send_sem=factor_send.at[level - 1],
            recv_sem=mate_recv.at[level - 1, n],
            device_id=(row, mate), device_id_type=MESH,
        )

    def factor_wait(level, first, count, strips, send, recv):
        piece = fulls[level - 1].at[pl.ds(first, count), pl.ds(0, strips * lines), :]
        return pltpu.make_async_remote_copy(
            src_ref=piece, dst_ref=piece, send_sem=send, recv_sem=recv,
            device_id=(row, mate), device_id_type=MESH,
        )

    def mask_factor(level):
        start = level * (level - 1) // 2

        def one(n, _):
            node = row * 2 + n
            size = sizes[level, node]
            above = node
            for up in range(level - 1, -1, -1):
                above = parents[up, above]
                upper = sizes[up, above]
                keep = (line_of < upper) & (column_of < size)
                block = jnp.where(keep, panel[start + up, n].astype(F32), 0.0)
                fulls[level - 1][
                    n * level + up, pl.ds(pl.multiple_of(col * lines, lines), lines), :
                ] = block.astype(BF16)
            return 0

        lax.fori_loop(0, 2, one, 0)

    def ring(level, step):
        for n in (0, 1):
            came = [way for way in (0, 1) if step > 0 and goes(n, way, step - 1)]
            if came:
                factor_wait(
                    level, n * level, level, len(came), factor_send.at[level - 1], ring_recv.at[level - 1, n, step - 1]
                ).wait_recv()
            for way in (0, 1):
                if goes(n, way, step):
                    ring_copy(level, n, way, step).start()
            if step == 0:
                mate_copy(level, n, 0, -1).start()
            for way in came:
                mate_copy(level, n, way, step - 1).start()

    def ring_end(level):
        for n in (0, 1):
            factor_wait(
                level, n * level, level, 8, factor_send.at[level - 1], mate_recv.at[level - 1, n]
            ).wait_recv()

    def ring_sent(level):
        factor_wait(
            level, 0, 2 * level, 15, factor_send.at[level - 1], mate_recv.at[level - 1, 0]
        ).wait_send()

    def chain_part(level, n, part, there):
        d = level
        first, count = ((0, d * d), (d * d, d), (d * d + d, d), (d * d + 2 * d, 1))[part]
        return cands[d].at[n + 2 if there else n, pl.ds(first, count)]

    def remote(src, dst, send, recv, place):
        return pltpu.make_async_remote_copy(
            src_ref=src, dst_ref=dst, send_sem=send, recv_sem=recv, device_id=place, device_id_type=MESH
        )

    def scale_part(level, n, part):
        first, count = (0, 3 * level) if part == 0 else (3 * level + part - 1, 1)
        if level == 0:
            first, count = 0, 3
        return scales[level].at[n, pl.ds(first, count)]

    def pass_on(level, n, part):
        place = (next_row, col)
        remote(
            scale_part(level, n, part), scale_part(level, n + 2, part),
            scale_send.at[level], scale_recv.at[level], place,
        ).start()
        remote(
            chain_part(level, n, part, False), chain_part(level, n, part, True),
            chain_send.at[level], chain_recv.at[level], place,
        ).start()

    def chain_all(level):
        ours, theirs, place = pl.ds(0, 2), pl.ds(2, 2), (next_row, col)
        return (
            remote(scales[level].at[ours], scales[level].at[theirs], scale_send.at[level], scale_recv.at[level], place),
            remote(cands[level].at[ours], cands[level].at[theirs], chain_send.at[level], chain_recv.at[level], place),
        )

    def turn_copies(level, slab, k):
        there = (col + k) % cols_n
        place = (row, there)
        return (
            remote(
                mark_out.at[level - 1, slab], mark_in.at[level - 1, slab, col],
                mark_send.at[level - 1, slab], mark_recv.at[level - 1, slab], place,
            ),
            remote(
                turn_out[level - 1].at[slab, there], turn_in[level - 1].at[slab, col],
                turn_send.at[level - 1, slab], turn_recv.at[level - 1, slab], place,
            ),
        )

    def turn_all(level, slab):
        most, place = pl.ds(0, cols_n - 1), (row, mate)
        marks = mark_in.at[level - 1, slab, most]
        pieces = turn_in[level - 1].at[slab, most]
        return (
            remote(marks, marks, mark_send.at[level - 1, slab], mark_recv.at[level - 1, slab], place),
            remote(pieces, pieces, turn_send.at[level - 1, slab], turn_recv.at[level - 1, slab], place),
        )

    def parts_of(level):
        return (3,) if level == 0 else (0, 1, 2, 3)

    def split(value):
        high = value.astype(BF16)
        return high, (value - high.astype(F32)).astype(BF16)

    lane_of = lax.broadcasted_iota(jnp.int32, (lines, 128), 1)
    per = 128 // lines
    sixteenth = lax.broadcasted_iota(jnp.int32, (16, 128), 0)

    def wide(scale):
        return jnp.concatenate([scale] * (width // 128), axis=1)

    def select_and_cross(level):
        d = level - 1
        start = level * (level - 1) // 2
        tall = lines * level

        def one(n, _):
            node = row * 2 + n
            parent = parents[d, node]
            own = (parent >= row * 2) & (parent < row * 2 + 2)
            slot = jnp.where(own, 0, 2) + lax.rem(parent, 2)
            table = scales[d][slot]
            if level < LEVELS - 1:
                scales[level][n, 0 : 3 * level] = table
            for l in range(level):
                for m in range(level):
                    if l < d and m < d:
                        entry = l * d + m
                    elif l < d:
                        entry = d * d + l
                    elif m < d:
                        entry = d * d + d + m
                    else:
                        entry = d * d + 2 * d
                    scale = table[3 * max(l, m) + (2 if l == m else 0 if l < m else 1)]
                    code = cands[d][slot, entry]
                    if level < LEVELS - 1:
                        cands[level][n, l * level + m] = code
                    high, low = split(decode(code.astype(F32)) * wide(scale))
                    lhs[m, l * lines : (l + 1) * lines, :] = high
                    lhs[m, tall + l * lines : tall + (l + 1) * lines, :] = low
            if level < LEVELS - 1:
                pass_on(level, n, 0)
            acc[0 : 2 * tall, :] = jnp.zeros((2 * tall, width), F32)

            def add(m, _):
                acc[0 : 2 * tall, :] += jnp.dot(
                    lhs[m, 0 : 2 * tall, :], fulls[level - 1][n * level + m], preferred_element_type=F32
                )
                return 0

            lax.fori_loop(0, level, add, 0)
            crossed = -(acc[0:tall, :] + acc[tall : 2 * tall, :])
            scale = scale_of(crossed)
            code = encode(crossed, scale)
            for l in range(level):
                cross_out[start + l, n] = crossed[l * lines : (l + 1) * lines, :]
                if level < LEVELS - 1:
                    cands[level][n, level * level + l] = code[l * lines : (l + 1) * lines, :].astype(BF16)
            if level < LEVELS - 1:
                scales[level][n, 3 * level] = jnp.broadcast_to(scale, (1, 128))
                pass_on(level, n, 1)
            turned = jnp.transpose(code, (1, 0)).astype(BF16)
            slab = 0 if joint(level) else n
            first = n * tall if joint(level) else 0
            for c in range(cols_n):
                turn_out[level - 1][slab, c, :, first : first + tall] = turned[
                    c * lines : (c + 1) * lines, :
                ]
            lane = lax.broadcasted_iota(jnp.int32, (1, 128), 1)
            mark = jnp.broadcast_to(scale, (1, 128))
            if joint(level) and n == 1:
                mark = jnp.where(lane < tall, mark_out[level - 1, 0], mark)
            mark_out[level - 1, slab] = mark
            if not joint(level):
                send_turn(level, n)
            return 0

        if joint(level):
            one(0, 0)
            one(1, 0)
            send_turn(level, 0)
        else:
            lax.fori_loop(0, 2, one, 0)

    def send_turn(level, slab):
        def send(k, _):
            for copy in turn_copies(level, slab, k):
                copy.start()
            return 0

        lax.fori_loop(1, cols_n, send, 0)
        turn_in[level - 1][slab, col] = turn_out[level - 1][slab, col]
        mark_in[level - 1, slab, col] = mark_out[level - 1, slab]

    def open_turn(level, slab):
        for copy in turn_all(level, slab):
            copy.wait_recv()
        lanes = lanes_of(level)

        def undo(c, _):
            code = turn_in[level - 1][slab, c].astype(F32)
            mark = jnp.concatenate([mark_in[level - 1, slab, c]] * (lanes // 128), axis=1)
            opened[c, :, 0:lanes] = decode(code) * mark
            return 0

        lax.fori_loop(0, cols_n, undo, 0)

    def finish_level(level):
        def one(n, _):
            if not joint(level):
                open_turn(level, n)
            for l in range(level):
                group = l + n * level if joint(level) else l
                for q in range(width // 128):
                    piece = None
                    for k in range(per):
                        source = opened[
                            q * per + k, :, (group // per) * 128 : (group // per) * 128 + 128
                        ]
                        shift = ((k - group % per) * lines) % 128
                        if shift:
                            source = pltpu.roll(source, shift, 1)
                        piece = source if piece is None else jnp.where(lane_of >= k * lines, source, piece)
                    high, low = split(piece)
                    lhs[l, 0:lines, q * 128 : (q + 1) * 128] = high
                    lhs[l, lines : 2 * lines, q * 128 : (q + 1) * 128] = low
                    if level < LEVELS - 1:
                        turned_f32[l * lines : (l + 1) * lines, q * 128 : (q + 1) * 128] = piece
            if level < LEVELS - 1:
                whole = turned_f32[0 : level * lines, :]
                scale = scale_of(whole)
                code = encode(whole, scale).astype(BF16)
                for l in range(level):
                    cands[level][n, level * level + level + l] = code[l * lines : (l + 1) * lines, :]
                scales[level][n, 3 * level + 1] = jnp.broadcast_to(scale, (1, 128))
                pass_on(level, n, 2)
            acc[0 : 2 * lines, :] = jnp.zeros((2 * lines, width), F32)

            def add(l, _):
                acc[0 : 2 * lines, :] += jnp.dot(
                    lhs[l, 0 : 2 * lines, :], fulls[level - 1][n * level + l], preferred_element_type=F32
                )
                return 0

            lax.fori_loop(0, level, add, 0)
            marginal = base_of(level, n) - (acc[0:lines, :] + acc[lines : 2 * lines, :])
            marg_out[level, n] = marginal
            if level < LEVELS - 1:
                send_marginal(level, n, marginal)
            return 0

        if joint(level):
            open_turn(level, 0)
            one(0, 0)
            one(1, 0)
        else:
            lax.fori_loop(0, 2, one, 0)

    def keep_marginal(level, n, marginal):
        scale = scale_of(marginal)
        cands[level][n, level * level + 2 * level] = encode(marginal, scale).astype(BF16)
        for entry in range(3) if level == 0 else (3 * level + 2,):
            scales[level][n, entry] = jnp.broadcast_to(scale, (1, 128))

    def send_marginal(level, n, marginal):
        keep_marginal(level, n, marginal)
        pass_on(level, n, 3)

    mask_factor(1)
    for n in range(2):
        marginal = base_of(0, n)
        marg_out[0, n] = marginal
        keep_marginal(0, n, marginal)
    for level in range(2, LEVELS):
        mask_factor(level)
    pl.semaphore_wait(barrier, cols_n + 1)
    ring(1, 0)
    pass_on(0, 0, 3)
    pass_on(0, 1, 3)
    for job in PREPARE:
        ring(*job)
    for level in range(1, LEVELS):
        for job in BEFORE[level]:
            ring(*job)
        ring_end(level)
        for copy in chain_all(level - 1):
            copy.wait_recv()
        select_and_cross(level)
        for job in MIDDLE[level]:
            ring(*job)
        finish_level(level)
        for job in AFTER[level]:
            ring(*job)

    for level in range(1, LEVELS):
        ring_sent(level)
        for slab in (0,) if joint(level) else (0, 1):
            for copy in turn_all(level, slab):
                copy.wait_send()
        for copy in chain_all(level - 1):
            copy.wait_send()


def solution(mesh):
    rows_n, cols_n = mesh.shape["row"], mesh.shape["col"]

    def shards(panel, diag_inverse, parents, sizes):
        pairs, per, lines, width = panel.shape
        vmem = pl.BlockSpec(memory_space=pltpu.VMEM)
        smem = pl.BlockSpec(memory_space=pltpu.SMEM)
        dma = pltpu.SemaphoreType.DMA

        def turn_shape(level):
            return (1 if joint(level) else 2, cols_n, lines, lanes_of(level))

        return pl.pallas_call(
            functools.partial(kernel, rows_n, cols_n),
            out_shape=(
                jax.ShapeDtypeStruct((pairs, per, lines, width), F32),
                jax.ShapeDtypeStruct((LEVELS, per, lines, width), F32),
            ),
            in_specs=[vmem, vmem, smem, smem],
            out_specs=(vmem, vmem),
            scratch_shapes=[
                *[pltpu.VMEM((4, (d + 1) * (d + 1), lines, width), BF16) for d in range(5)],
                *[pltpu.VMEM((2 * d, width, width), BF16) for d in range(1, 6)],
                *[pltpu.VMEM(turn_shape(d), BF16) for d in range(1, 6)],
                *[pltpu.VMEM(turn_shape(d), BF16) for d in range(1, 6)],
                *[pltpu.VMEM((4, 3 * (d + 1), 1, 128), F32) for d in range(5)],
                pltpu.VMEM((5, 320, width), BF16),
                pltpu.VMEM((320, width), F32),
                pltpu.VMEM((cols_n, lines, 256), F32),
                pltpu.VMEM((4 * lines, width), F32),
                pltpu.VMEM((5, 2, 1, 128), F32),
                pltpu.VMEM((5, 2, cols_n, 1, 128), F32),
                dma((5,)),
                dma((5, 2, 4)),
                dma((5, 2)),
                dma((5,)),
                dma((5,)),
                dma((5,)),
                dma((5,)),
                dma((5, 2)),
                dma((5, 2)),
                dma((5, 2)),
                dma((5, 2)),
            ],
            compiler_params=pltpu.CompilerParams(
                collective_id=0, has_side_effects=True, vmem_limit_bytes=64000 * 1024
            ),
        )(panel, diag_inverse, parents, sizes)

    in_specs = (P(None, "row", "col", None), P(None, "row", "col", None), P(), P())
    out_specs = (P(None, "row", "col", None), P(None, "row", "col", None))
    return jax.shard_map(shards, mesh=mesh, in_specs=in_specs, out_specs=out_specs, check_vma=False)
```

```python
import functools

import jax
import jax.numpy as jnp
from jax import lax
from jax.experimental import pallas as pl
from jax.experimental.pallas import tpu as pltpu
from jax.sharding import PartitionSpec as P

MESH = pl.DeviceIdType.MESH
LEVELS = 6
F32 = jnp.float32
BF16 = jnp.bfloat16


POWER = 6
PREPARE = ((2, 0), (1, 1), (2, 1), (1, 2), (2, 2), (1, 3), (2, 3), (3, 0), (1, 4))
BEFORE = {1: (), 2: ((3, 3), (4, 0)), 3: ((4, 2),), 4: ((4, 4), (5, 1)), 5: ((5, 4),)}
MIDDLE = {1: ((2, 4), (3, 1)), 2: ((3, 4), (4, 1)), 3: ((4, 3), (5, 0)), 4: ((5, 2), (5, 3)), 5: ()}
AFTER = {1: ((3, 2),), 2: (), 3: (), 4: (), 5: ()}


def joint(level):
    return level <= 2


def lanes_of(level):
    tall = 32 * level * (2 if joint(level) else 1)
    return 128 * (-(-tall // 128))


def scale_of(value):
    top = jnp.max(jnp.max(jnp.abs(value), axis=0, keepdims=True), axis=1, keepdims=True)
    return jnp.maximum(top, 1e-30).astype(BF16).astype(F32)


def encode(value, scale):
    unit = value * (1.0 / scale)
    square = unit * unit
    return unit * jnp.abs(unit) * (square * square)


def decode(code):
    root = jnp.exp(jnp.log(jnp.abs(code)) * (1.0 / POWER))
    return jnp.where(code > 0.0, root, jnp.where(code < 0.0, -root, 0.0))


def kernel(rows_n, cols_n, panel, diag, parents, sizes, cross_out, marg_out, *scratch):
    cands = scratch[0:5]
    fulls = scratch[5:10]
    turn_out = scratch[10:15]
    turn_in = scratch[15:20]
    scales = scratch[20:25]
    (
        lhs, opened, turned_f32, mark_out, mark_in, factor_send, ring_recv, mate_recv,
        chain_send, chain_recv, scale_send, scale_recv, turn_send, turn_recv, mark_send, mark_recv,
    ) = scratch[25:]
    width = diag.shape[3]
    lines = diag.shape[2]
    chips = cols_n // 2
    row = lax.axis_index("row")
    col = lax.axis_index("col")
    chip = col // 2
    core = col % 2
    mate = col + 1 - 2 * core
    right = (col + 2) % cols_n
    left = (col + cols_n - 2) % cols_n
    next_row = (row + 1) % rows_n
    prev_row = (row + rows_n - 1) % rows_n

    barrier = pltpu.get_barrier_semaphore()
    for k in range(1, cols_n):
        pl.semaphore_signal(barrier, inc=1, device_id=(row, (col + k) % cols_n), device_id_type=MESH)
    pl.semaphore_signal(barrier, inc=1, device_id=(next_row, col), device_id_type=MESH)
    pl.semaphore_signal(barrier, inc=1, device_id=(prev_row, col), device_id_type=MESH)
    line_of = lax.broadcasted_iota(jnp.int32, (lines, width), 0) + col * lines
    column_of = lax.broadcasted_iota(jnp.int32, (lines, width), 1)

    def base_of(level, n):
        size = sizes[level, row * 2 + n]
        live = (line_of < size) & (column_of < size)
        eye = (line_of == column_of) & (line_of >= size)
        return jnp.where(live, diag[level, n], jnp.where(eye, 1.0, 0.0))

    def strip(level, at, first, count):
        return fulls[level - 1].at[
            pl.ds(first, count), pl.ds(pl.multiple_of(at * lines, lines), lines), :
        ]

    def goes(n, way, step):
        return step < 3 or (step == 3 and way == n)

    def ring_copy(level, n, way, step):
        at = ((chip - step + chips) % chips if way == 0 else (chip + step) % chips) * 2 + core
        piece = strip(level, at, n * level, level)
        return pltpu.make_async_remote_copy(
            src_ref=piece, dst_ref=piece,
            send_sem=factor_send.at[level - 1],
            recv_sem=ring_recv.at[level - 1, n, step],
            device_id=(row, right if way == 0 else left), device_id_type=MESH,
        )

    def mate_copy(level, n, way, step):
        if step < 0:
            at = chip
        else:
            at = (chip - step - 1 + chips) % chips if way == 0 else (chip + step + 1) % chips
        piece = strip(level, at * 2 + core, n * level, level)
        return pltpu.make_async_remote_copy(
            src_ref=piece, dst_ref=piece,
            send_sem=factor_send.at[level - 1],
            recv_sem=mate_recv.at[level - 1, n],
            device_id=(row, mate), device_id_type=MESH,
        )

    def factor_wait(level, first, count, strips, send, recv):
        piece = fulls[level - 1].at[pl.ds(first, count), pl.ds(0, strips * lines), :]
        return pltpu.make_async_remote_copy(
            src_ref=piece, dst_ref=piece, send_sem=send, recv_sem=recv,
            device_id=(row, mate), device_id_type=MESH,
        )

    def mask_factor(level):
        start = level * (level - 1) // 2

        def one(n, _):
            node = row * 2 + n
            size = sizes[level, node]
            above = node
            for up in range(level - 1, -1, -1):
                above = parents[up, above]
                upper = sizes[up, above]
                keep = (line_of < upper) & (column_of < size)
                block = jnp.where(keep, panel[start + up, n].astype(F32), 0.0)
                fulls[level - 1][
                    n * level + up, pl.ds(pl.multiple_of(col * lines, lines), lines), :
                ] = block.astype(BF16)
            return 0

        lax.fori_loop(0, 2, one, 0)

    def ring(level, step):
        for n in (0, 1):
            came = [way for way in (0, 1) if step > 0 and goes(n, way, step - 1)]
            if came:
                factor_wait(
                    level, n * level, level, len(came), factor_send.at[level - 1], ring_recv.at[level - 1, n, step - 1]
                ).wait_recv()
            for way in (0, 1):
                if goes(n, way, step):
                    ring_copy(level, n, way, step).start()
            if step == 0:
                mate_copy(level, n, 0, -1).start()
            for way in came:
                mate_copy(level, n, way, step - 1).start()

    def ring_end(level):
        for n in (0, 1):
            factor_wait(
                level, n * level, level, 8, factor_send.at[level - 1], mate_recv.at[level - 1, n]
            ).wait_recv()

    def ring_sent(level):
        factor_wait(
            level, 0, 2 * level, 15, factor_send.at[level - 1], mate_recv.at[level - 1, 0]
        ).wait_send()

    def chain_part(level, n, part, there):
        d = level
        first, count = ((0, d * d), (d * d, d), (d * d + d, d), (d * d + 2 * d, 1))[part]
        return cands[d].at[n + 2 if there else n, pl.ds(first, count)]

    def remote(src, dst, send, recv, place):
        return pltpu.make_async_remote_copy(
            src_ref=src, dst_ref=dst, send_sem=send, recv_sem=recv, device_id=place, device_id_type=MESH
        )

    def scale_part(level, n, part):
        first, count = (0, 3 * level) if part == 0 else (3 * level + part - 1, 1)
        if level == 0:
            first, count = 0, 3
        return scales[level].at[n, pl.ds(first, count)]

    def pass_on(level, n, part):
        place = (next_row, col)
        remote(
            scale_part(level, n, part), scale_part(level, n + 2, part),
            scale_send.at[level], scale_recv.at[level], place,
        ).start()
        remote(
            chain_part(level, n, part, False), chain_part(level, n, part, True),
            chain_send.at[level], chain_recv.at[level], place,
        ).start()

    def chain_all(level):
        ours, theirs, place = pl.ds(0, 2), pl.ds(2, 2), (next_row, col)
        return (
            remote(scales[level].at[ours], scales[level].at[theirs], scale_send.at[level], scale_recv.at[level], place),
            remote(cands[level].at[ours], cands[level].at[theirs], chain_send.at[level], chain_recv.at[level], place),
        )

    def turn_copies(level, slab, k):
        there = (col + k) % cols_n
        place = (row, there)
        return (
            remote(
                mark_out.at[level - 1, slab], mark_in.at[level - 1, slab, col],
                mark_send.at[level - 1, slab], mark_recv.at[level - 1, slab], place,
            ),
            remote(
                turn_out[level - 1].at[slab, there], turn_in[level - 1].at[slab, col],
                turn_send.at[level - 1, slab], turn_recv.at[level - 1, slab], place,
            ),
        )

    def turn_all(level, slab):
        most, place = pl.ds(0, cols_n - 1), (row, mate)
        marks = mark_in.at[level - 1, slab, most]
        pieces = turn_in[level - 1].at[slab, most]
        return (
            remote(marks, marks, mark_send.at[level - 1, slab], mark_recv.at[level - 1, slab], place),
            remote(pieces, pieces, turn_send.at[level - 1, slab], turn_recv.at[level - 1, slab], place),
        )

    def parts_of(level):
        return (3,) if level == 0 else (0, 1, 2, 3)

    def split(value):
        high = value.astype(BF16)
        return high, (value - high.astype(F32)).astype(BF16)

    lane_of = lax.broadcasted_iota(jnp.int32, (lines, 128), 1)
    per = 128 // lines
    sixteenth = lax.broadcasted_iota(jnp.int32, (16, 128), 0)

    def wide(scale):
        return jnp.concatenate([scale] * (width // 128), axis=1)

    def select_and_cross(level):
        d = level - 1
        start = level * (level - 1) // 2
        tall = lines * level

        def one(n, _):
            node = row * 2 + n
            parent = parents[d, node]
            own = (parent >= row * 2) & (parent < row * 2 + 2)
            slot = jnp.where(own, 0, 2) + lax.rem(parent, 2)
            table = scales[d][slot]
            if level < LEVELS - 1:
                scales[level][n, 0 : 3 * level] = table
            for l in range(level):
                for m in range(level):
                    if l < d and m < d:
                        entry = l * d + m
                    elif l < d:
                        entry = d * d + l
                    elif m < d:
                        entry = d * d + d + m
                    else:
                        entry = d * d + 2 * d
                    scale = table[3 * max(l, m) + (2 if l == m else 0 if l < m else 1)]
                    code = cands[d][slot, entry]
                    if level < LEVELS - 1:
                        cands[level][n, l * level + m] = code
                    high, low = split(decode(code.astype(F32)) * wide(scale))
                    lhs[l * lines : (l + 1) * lines, m * width : (m + 1) * width] = high
                    lhs[tall + l * lines : tall + (l + 1) * lines, m * width : (m + 1) * width] = low
            if level < LEVELS - 1:
                pass_on(level, n, 0)
            both = jnp.dot(
                lhs[0 : 2 * tall, 0 : level * width],
                fulls[level - 1][pl.ds(n * level, level)].reshape(level * width, width),
                preferred_element_type=F32,
            )
            crossed = -(both[0:tall, :] + both[tall : 2 * tall, :])
            scale = scale_of(crossed)
            code = encode(crossed, scale)
            for l in range(level):
                cross_out[start + l, n] = crossed[l * lines : (l + 1) * lines, :]
                if level < LEVELS - 1:
                    cands[level][n, level * level + l] = code[l * lines : (l + 1) * lines, :].astype(BF16)
            if level < LEVELS - 1:
                scales[level][n, 3 * level] = jnp.broadcast_to(scale, (1, 128))
                pass_on(level, n, 1)
            turned = jnp.transpose(code, (1, 0)).astype(BF16)
            slab = 0 if joint(level) else n
            first = n * tall if joint(level) else 0
            for c in range(cols_n):
                turn_out[level - 1][slab, c, :, first : first + tall] = turned[
                    c * lines : (c + 1) * lines, :
                ]
            lane = lax.broadcasted_iota(jnp.int32, (1, 128), 1)
            mark = jnp.broadcast_to(scale, (1, 128))
            if joint(level) and n == 1:
                mark = jnp.where(lane < tall, mark_out[level - 1, 0], mark)
            mark_out[level - 1, slab] = mark
            if not joint(level):
                send_turn(level, n)
            return 0

        if joint(level):
            one(0, 0)
            one(1, 0)
            send_turn(level, 0)
        else:
            lax.fori_loop(0, 2, one, 0)

    def send_turn(level, slab):
        def send(k, _):
            for copy in turn_copies(level, slab, k):
                copy.start()
            return 0

        lax.fori_loop(1, cols_n, send, 0)
        turn_in[level - 1][slab, col] = turn_out[level - 1][slab, col]
        mark_in[level - 1, slab, col] = mark_out[level - 1, slab]

    def open_turn(level, slab):
        for copy in turn_all(level, slab):
            copy.wait_recv()
        lanes = lanes_of(level)

        def undo(c, _):
            code = turn_in[level - 1][slab, c].astype(F32)
            mark = jnp.concatenate([mark_in[level - 1, slab, c]] * (lanes // 128), axis=1)
            opened[c, :, 0:lanes] = decode(code) * mark
            return 0

        lax.fori_loop(0, cols_n, undo, 0)

    def finish_level(level):
        def one(n, _):
            if not joint(level):
                open_turn(level, n)
            for l in range(level):
                group = l + n * level if joint(level) else l
                for q in range(width // 128):
                    piece = None
                    for k in range(per):
                        source = opened[
                            q * per + k, :, (group // per) * 128 : (group // per) * 128 + 128
                        ]
                        shift = ((k - group % per) * lines) % 128
                        if shift:
                            source = pltpu.roll(source, shift, 1)
                        piece = source if piece is None else jnp.where(lane_of >= k * lines, source, piece)
                    high, low = split(piece)
                    lhs[0:lines, l * width + q * 128 : l * width + (q + 1) * 128] = high
                    lhs[lines : 2 * lines, l * width + q * 128 : l * width + (q + 1) * 128] = low
                    if level < LEVELS - 1:
                        turned_f32[l * lines : (l + 1) * lines, q * 128 : (q + 1) * 128] = piece
            if level < LEVELS - 1:
                whole = turned_f32[0 : level * lines, :]
                scale = scale_of(whole)
                code = encode(whole, scale).astype(BF16)
                for l in range(level):
                    cands[level][n, level * level + level + l] = code[l * lines : (l + 1) * lines, :]
                scales[level][n, 3 * level + 1] = jnp.broadcast_to(scale, (1, 128))
                pass_on(level, n, 2)
            both = jnp.dot(
                lhs[0 : 2 * lines, 0 : level * width],
                fulls[level - 1][pl.ds(n * level, level)].reshape(level * width, width),
                preferred_element_type=F32,
            )
            marginal = base_of(level, n) - (both[0:lines, :] + both[lines : 2 * lines, :])
            marg_out[level, n] = marginal
            if level < LEVELS - 1:
                send_marginal(level, n, marginal)
            return 0

        if joint(level):
            open_turn(level, 0)
            one(0, 0)
            one(1, 0)
        else:
            lax.fori_loop(0, 2, one, 0)

    def keep_marginal(level, n, marginal):
        scale = scale_of(marginal)
        cands[level][n, level * level + 2 * level] = encode(marginal, scale).astype(BF16)
        for entry in range(3) if level == 0 else (3 * level + 2,):
            scales[level][n, entry] = jnp.broadcast_to(scale, (1, 128))

    def send_marginal(level, n, marginal):
        keep_marginal(level, n, marginal)
        pass_on(level, n, 3)

    mask_factor(1)
    for n in range(2):
        marginal = base_of(0, n)
        marg_out[0, n] = marginal
        keep_marginal(0, n, marginal)
    for level in range(2, LEVELS):
        mask_factor(level)
    pl.semaphore_wait(barrier, cols_n + 1)
    ring(1, 0)
    pass_on(0, 0, 3)
    pass_on(0, 1, 3)
    for job in PREPARE:
        ring(*job)
    for level in range(1, LEVELS):
        for job in BEFORE[level]:
            ring(*job)
        ring_end(level)
        for copy in chain_all(level - 1):
            copy.wait_recv()
        select_and_cross(level)
        for job in MIDDLE[level]:
            ring(*job)
        finish_level(level)
        for job in AFTER[level]:
            ring(*job)

    for level in range(1, LEVELS):
        ring_sent(level)
        for slab in (0,) if joint(level) else (0, 1):
            for copy in turn_all(level, slab):
                copy.wait_send()
        for copy in chain_all(level - 1):
            copy.wait_send()


def solution(mesh):
    rows_n, cols_n = mesh.shape["row"], mesh.shape["col"]

    def shards(panel, diag_inverse, parents, sizes):
        pairs, per, lines, width = panel.shape
        vmem = pl.BlockSpec(memory_space=pltpu.VMEM)
        smem = pl.BlockSpec(memory_space=pltpu.SMEM)
        dma = pltpu.SemaphoreType.DMA

        def turn_shape(level):
            return (1 if joint(level) else 2, cols_n, lines, lanes_of(level))

        return pl.pallas_call(
            functools.partial(kernel, rows_n, cols_n),
            out_shape=(
                jax.ShapeDtypeStruct((pairs, per, lines, width), F32),
                jax.ShapeDtypeStruct((LEVELS, per, lines, width), F32),
            ),
            in_specs=[vmem, vmem, smem, smem],
            out_specs=(vmem, vmem),
            scratch_shapes=[
                *[pltpu.VMEM((4, (d + 1) * (d + 1), lines, width), BF16) for d in range(5)],
                *[pltpu.VMEM((2 * d, width, width), BF16) for d in range(1, 6)],
                *[pltpu.VMEM(turn_shape(d), BF16) for d in range(1, 6)],
                *[pltpu.VMEM(turn_shape(d), BF16) for d in range(1, 6)],
                *[pltpu.VMEM((4, 3 * (d + 1), 1, 128), F32) for d in range(5)],
                pltpu.VMEM((320, 5 * width), BF16),
                pltpu.VMEM((cols_n, lines, 256), F32),
                pltpu.VMEM((4 * lines, width), F32),
                pltpu.VMEM((5, 2, 1, 128), F32),
                pltpu.VMEM((5, 2, cols_n, 1, 128), F32),
                dma((5,)),
                dma((5, 2, 4)),
                dma((5, 2)),
                dma((5,)),
                dma((5,)),
                dma((5,)),
                dma((5,)),
                dma((5, 2)),
                dma((5, 2)),
                dma((5, 2)),
                dma((5, 2)),
            ],
            compiler_params=pltpu.CompilerParams(
                collective_id=0, has_side_effects=True, vmem_limit_bytes=44000 * 1024
            ),
        )(panel, diag_inverse, parents, sizes)

    in_specs = (P(None, "row", "col", None), P(None, "row", "col", None), P(), P())
    out_specs = (P(None, "row", "col", None), P(None, "row", "col", None))
    return jax.shard_map(shards, mesh=mesh, in_specs=in_specs, out_specs=out_specs, check_vma=False)
```

```python
import functools

import jax
import jax.numpy as jnp
from jax import lax
from jax.experimental import pallas as pl
from jax.experimental.pallas import tpu as pltpu
from jax.sharding import PartitionSpec as P

MESH = pl.DeviceIdType.MESH
LEVELS = 6
F32 = jnp.float32
BF16 = jnp.bfloat16


POWER = 6
PREPARE = ((2, 0), (1, 1), (2, 1), (1, 2), (2, 2), (1, 3), (2, 3), (3, 0), (1, 4))
BEFORE = {
    1: (),
    2: ((3, 3), (4, 0)),
    3: ((4, 2),),
    4: ((4, 4), (5, 1, (0,)), (5, 0, (1,))),
    5: ((5, 4, (0,)), (5, 3, (1,))),
}
FIRST = {
    1: (("pass", 0, 1),),
    2: (("pass", 1, 1), ("pass", 0, 4)),
    3: (("pass", 2, 1),),
    4: (("pass", 3, 1),),
    5: (),
}
BETWEEN = ((5, 4, (1,)),)
MIDDLE = {
    1: (("pass", 0, 2), (2, 4), (3, 1)),
    2: (("pass", 1, 2), (3, 4), (4, 1)),
    3: (("pass", 2, 2), (4, 3), (5, 0, (0,))),
    4: ((5, 2, (0,)), (5, 1, (1,)), (5, 3, (0,)), (5, 2, (1,))),
    5: (),
}
AFTER = {1: (("pass", 0, 3), (3, 2)), 2: (("pass", 1, 3),), 3: (), 4: (), 5: ()}
HOPS = tuple((level, k) for level in range(5) for k in range(6 - level))
SENDS = tuple((level, k) for level in range(5) for k in range(5 - level))


def joint(level):
    return level <= 2


def lanes_of(level):
    tall = 32 * level * (2 if joint(level) else 1)
    return 128 * (-(-tall // 128))


def scale_of(value):
    top = jnp.max(jnp.max(jnp.abs(value), axis=0, keepdims=True), axis=1, keepdims=True)
    return jnp.maximum(top, 1e-30).astype(BF16).astype(F32)


def encode(value, scale):
    unit = value * (1.0 / scale)
    square = unit * unit
    return unit * jnp.abs(unit) * (square * square)


def decode(code):
    root = jnp.exp(jnp.log(jnp.abs(code)) * (1.0 / POWER))
    return jnp.where(code > 0.0, root, jnp.where(code < 0.0, -root, 0.0))


def kernel(rows_n, cols_n, panel, diag, parents, sizes, cross_out, marg_out, *scratch):
    fulls = scratch[0:5]
    turn_out = scratch[5:10]
    turn_in = scratch[10:15]
    blocks = {place: scratch[15 + at] for at, place in enumerate(HOPS)}
    marks = {place: scratch[15 + len(HOPS) + at] for at, place in enumerate(HOPS)}
    (
        lhs, opened, turned_f32, mark_out, mark_in, factor_send, ring_recv, mate_recv,
        chain_send, chain_recv, scale_send, scale_recv, turn_send, turn_recv, mark_send, mark_recv,
    ) = scratch[15 + 2 * len(HOPS) :]
    width = diag.shape[3]
    lines = diag.shape[2]
    chips = cols_n // 2
    row = lax.axis_index("row")
    col = lax.axis_index("col")
    chip = col // 2
    core = col % 2
    mate = col + 1 - 2 * core
    right = (col + 2) % cols_n
    left = (col + cols_n - 2) % cols_n
    next_row = (row + 1) % rows_n
    prev_row = (row + rows_n - 1) % rows_n

    barrier = pltpu.get_barrier_semaphore()
    for k in range(1, cols_n):
        pl.semaphore_signal(barrier, inc=1, device_id=(row, (col + k) % cols_n), device_id_type=MESH)
    pl.semaphore_signal(barrier, inc=1, device_id=(next_row, col), device_id_type=MESH)
    pl.semaphore_signal(barrier, inc=1, device_id=(prev_row, col), device_id_type=MESH)
    line_of = lax.broadcasted_iota(jnp.int32, (lines, width), 0) + col * lines
    column_of = lax.broadcasted_iota(jnp.int32, (lines, width), 1)

    def base_of(level, n):
        size = sizes[level, row * 2 + n]
        live = (line_of < size) & (column_of < size)
        eye = (line_of == column_of) & (line_of >= size)
        return jnp.where(live, diag[level, n], jnp.where(eye, 1.0, 0.0))

    def strip(level, at, first, count):
        return fulls[level - 1].at[
            pl.ds(first, count), pl.ds(pl.multiple_of(at * lines, lines), lines), :
        ]

    def goes(n, way, step):
        return step < 3 or (step == 3 and way == n)

    def ring_copy(level, n, way, step):
        at = ((chip - step + chips) % chips if way == 0 else (chip + step) % chips) * 2 + core
        piece = strip(level, at, n * level, level)
        return pltpu.make_async_remote_copy(
            src_ref=piece, dst_ref=piece,
            send_sem=factor_send.at[level - 1],
            recv_sem=ring_recv.at[level - 1, n, step],
            device_id=(row, right if way == 0 else left), device_id_type=MESH,
        )

    def mate_copy(level, n, way, step):
        if step < 0:
            at = chip
        else:
            at = (chip - step - 1 + chips) % chips if way == 0 else (chip + step + 1) % chips
        piece = strip(level, at * 2 + core, n * level, level)
        return pltpu.make_async_remote_copy(
            src_ref=piece, dst_ref=piece,
            send_sem=factor_send.at[level - 1],
            recv_sem=mate_recv.at[level - 1, n],
            device_id=(row, mate), device_id_type=MESH,
        )

    def factor_wait(level, first, count, strips, send, recv):
        piece = fulls[level - 1].at[pl.ds(first, count), pl.ds(0, strips * lines), :]
        return pltpu.make_async_remote_copy(
            src_ref=piece, dst_ref=piece, send_sem=send, recv_sem=recv,
            device_id=(row, mate), device_id_type=MESH,
        )

    def mask_factor(level):
        start = level * (level - 1) // 2

        def one(n, _):
            node = row * 2 + n
            size = sizes[level, node]
            above = node
            for up in range(level - 1, -1, -1):
                above = parents[up, above]
                upper = sizes[up, above]
                keep = (line_of < upper) & (column_of < size)
                block = jnp.where(keep, panel[start + up, n].astype(F32), 0.0)
                fulls[level - 1][
                    n * level + up, pl.ds(pl.multiple_of(col * lines, lines), lines), :
                ] = block.astype(BF16)
            return 0

        lax.fori_loop(0, 2, one, 0)

    def ring(level, step, nodes=(0, 1)):
        for n in nodes:
            came = [way for way in (0, 1) if step > 0 and goes(n, way, step - 1)]
            if came:
                factor_wait(
                    level, n * level, level, len(came), factor_send.at[level - 1], ring_recv.at[level - 1, n, step - 1]
                ).wait_recv()
            for way in (0, 1):
                if goes(n, way, step):
                    ring_copy(level, n, way, step).start()
            if step == 0:
                mate_copy(level, n, 0, -1).start()
            for way in came:
                mate_copy(level, n, way, step - 1).start()

    def ring_end(level, n):
        factor_wait(
            level, n * level, level, 8, factor_send.at[level - 1], mate_recv.at[level - 1, n]
        ).wait_recv()

    def ring_sent(level):
        factor_wait(
            level, 0, 2 * level, 15, factor_send.at[level - 1], mate_recv.at[level - 1, 0]
        ).wait_send()

    def remote(src, dst, send, recv, place):
        return pltpu.make_async_remote_copy(
            src_ref=src, dst_ref=dst, send_sem=send, recv_sem=recv, device_id=place, device_id_type=MESH
        )

    def pass_on(level, n, part):
        place, at = (next_row, col), SENDS.index((level, 0))
        mark = pl.ds(0, 3) if level == 0 else pl.ds(part, 1)
        span = (pl.ds(0, level), pl.ds(level, level), pl.ds(2 * level, 1))[part]
        here, there = (level, 0), (level, 1)
        remote(
            marks[here].at[n, mark], marks[there].at[n, mark], scale_send.at[at], scale_recv.at[at], place
        ).start()
        remote(
            blocks[here].at[n, span], blocks[there].at[n, span], chain_send.at[at], chain_recv.at[at], place
        ).start()

    def hop(level, k):
        place, at = (next_row, col), SENDS.index((level, k))
        here, there = (level, k), (level, k + 1)
        return (
            remote(marks[here], marks[there], scale_send.at[at], scale_recv.at[at], place),
            remote(blocks[here], blocks[there], chain_send.at[at], chain_recv.at[at], place),
        )

    arrived = set()

    def receive(level, k):
        if (level, k) not in arrived:
            arrived.add((level, k))
            for copy in hop(level, k - 1):
                copy.wait_recv()

    def forward(level, k):
        receive(level, k)
        for copy in hop(level, k):
            copy.start()

    def turn_copies(level, slab, k):
        there = (col + k) % cols_n
        place = (row, there)
        return (
            remote(
                mark_out.at[level - 1, slab], mark_in.at[level - 1, slab, col],
                mark_send.at[level - 1, slab], mark_recv.at[level - 1, slab], place,
            ),
            remote(
                turn_out[level - 1].at[slab, there], turn_in[level - 1].at[slab, col],
                turn_send.at[level - 1, slab], turn_recv.at[level - 1, slab], place,
            ),
        )

    def turn_all(level, slab):
        most, place = pl.ds(0, cols_n - 1), (row, mate)
        marks = mark_in.at[level - 1, slab, most]
        pieces = turn_in[level - 1].at[slab, most]
        return (
            remote(marks, marks, mark_send.at[level - 1, slab], mark_recv.at[level - 1, slab], place),
            remote(pieces, pieces, turn_send.at[level - 1, slab], turn_recv.at[level - 1, slab], place),
        )

    def split(value):
        high = value.astype(BF16)
        return high, (value - high.astype(F32)).astype(BF16)

    lane_of = lax.broadcasted_iota(jnp.int32, (lines, 128), 1)
    per = 128 // lines
    sixteenth = lax.broadcasted_iota(jnp.int32, (16, 128), 0)

    def wide(scale):
        return jnp.concatenate([scale] * (width // 128), axis=1)

    def select_and_cross(level, nodes):
        start = level * (level - 1) // 2
        tall = lines * level

        def one(n, _):
            above = row * 2 + n
            within, distance = [None] * level, [None] * level
            for up in range(level - 1, -1, -1):
                above = parents[up, above]
                within[up] = lax.rem(above, 2)
                distance[up] = lax.rem(row + rows_n - lax.div(above, 2), rows_n)

            def pick(refs, up, entry):
                value = None
                for k in range(level - up + 1):
                    ref = refs[(up, k)]
                    there = ref[within[up]] if entry is None else ref[within[up], entry]
                    value = there if value is None else lax.select(distance[up] == k, there, value)
                return value

            table = [pick(marks, up, None) for up in range(level)]
            for l in range(level):
                for m in range(level):
                    up = max(l, m)
                    if l == m:
                        entry, which = 2 * up, 2
                    elif l < m:
                        entry, which = l, 0
                    else:
                        entry, which = up + m, 1
                    code = pick(blocks, up, entry)
                    high, low = split(decode(code.astype(F32)) * wide(table[up][which]))
                    lhs[l * lines : (l + 1) * lines, m * width : (m + 1) * width] = high
                    lhs[tall + l * lines : tall + (l + 1) * lines, m * width : (m + 1) * width] = low
            both = jnp.dot(
                lhs[0 : 2 * tall, 0 : level * width],
                fulls[level - 1][pl.ds(n * level, level)].reshape(level * width, width),
                preferred_element_type=F32,
            )
            crossed = -(both[0:tall, :] + both[tall : 2 * tall, :])
            scale = scale_of(crossed)
            code = encode(crossed, scale)
            for l in range(level):
                cross_out[start + l, n] = crossed[l * lines : (l + 1) * lines, :]
                if level < LEVELS - 1:
                    blocks[(level, 0)][n, l] = code[l * lines : (l + 1) * lines, :].astype(BF16)
            if level < LEVELS - 1:
                marks[(level, 0)][n, 0] = jnp.broadcast_to(scale, (1, 128))
                pass_on(level, n, 0)
            turned = jnp.transpose(code, (1, 0)).astype(BF16)
            slab = 0 if joint(level) else n
            first = n * tall if joint(level) else 0
            for c in range(cols_n):
                turn_out[level - 1][slab, c, :, first : first + tall] = turned[
                    c * lines : (c + 1) * lines, :
                ]
            lane = lax.broadcasted_iota(jnp.int32, (1, 128), 1)
            mark = jnp.broadcast_to(scale, (1, 128))
            if joint(level) and n == 1:
                mark = jnp.where(lane < tall, mark_out[level - 1, 0], mark)
            mark_out[level - 1, slab] = mark
            if not joint(level):
                send_turn(level, n)
            return 0

        if joint(level):
            one(0, 0)
            one(1, 0)
            send_turn(level, 0)
        elif len(nodes) == 1:
            one(nodes[0], 0)
        else:
            lax.fori_loop(0, 2, one, 0)

    def send_turn(level, slab):
        def send(k, _):
            for copy in turn_copies(level, slab, k):
                copy.start()
            return 0

        lax.fori_loop(1, cols_n, send, 0)
        turn_in[level - 1][slab, col] = turn_out[level - 1][slab, col]
        mark_in[level - 1, slab, col] = mark_out[level - 1, slab]

    def open_turn(level, slab):
        for copy in turn_all(level, slab):
            copy.wait_recv()
        lanes = lanes_of(level)

        def undo(c, _):
            code = turn_in[level - 1][slab, c].astype(F32)
            mark = jnp.concatenate([mark_in[level - 1, slab, c]] * (lanes // 128), axis=1)
            opened[c, :, 0:lanes] = decode(code) * mark
            return 0

        lax.fori_loop(0, cols_n, undo, 0)

    def finish_level(level):
        def one(n, _):
            if not joint(level):
                open_turn(level, n)
            for l in range(level):
                group = l + n * level if joint(level) else l
                for q in range(width // 128):
                    piece = None
                    for k in range(per):
                        source = opened[
                            q * per + k, :, (group // per) * 128 : (group // per) * 128 + 128
                        ]
                        shift = ((k - group % per) * lines) % 128
                        if shift:
                            source = pltpu.roll(source, shift, 1)
                        piece = source if piece is None else jnp.where(lane_of >= k * lines, source, piece)
                    high, low = split(piece)
                    lhs[0:lines, l * width + q * 128 : l * width + (q + 1) * 128] = high
                    lhs[lines : 2 * lines, l * width + q * 128 : l * width + (q + 1) * 128] = low
                    if level < LEVELS - 1:
                        turned_f32[l * lines : (l + 1) * lines, q * 128 : (q + 1) * 128] = piece
            if level < LEVELS - 1:
                whole = turned_f32[0 : level * lines, :]
                scale = scale_of(whole)
                code = encode(whole, scale).astype(BF16)
                for l in range(level):
                    blocks[(level, 0)][n, level + l] = code[l * lines : (l + 1) * lines, :]
                marks[(level, 0)][n, 1] = jnp.broadcast_to(scale, (1, 128))
                pass_on(level, n, 1)
            both = jnp.dot(
                lhs[0 : 2 * lines, 0 : level * width],
                fulls[level - 1][pl.ds(n * level, level)].reshape(level * width, width),
                preferred_element_type=F32,
            )
            marginal = base_of(level, n) - (both[0:lines, :] + both[lines : 2 * lines, :])
            marg_out[level, n] = marginal
            if level < LEVELS - 1:
                send_marginal(level, n, marginal)
            return 0

        if joint(level):
            open_turn(level, 0)
            one(0, 0)
            one(1, 0)
        else:
            lax.fori_loop(0, 2, one, 0)

    def keep_marginal(level, n, marginal):
        scale = scale_of(marginal)
        blocks[(level, 0)][n, 2 * level] = encode(marginal, scale).astype(BF16)
        for entry in range(3) if level == 0 else (2,):
            marks[(level, 0)][n, entry] = jnp.broadcast_to(scale, (1, 128))

    def send_marginal(level, n, marginal):
        keep_marginal(level, n, marginal)
        pass_on(level, n, 2)

    mask_factor(1)
    for n in range(2):
        marginal = base_of(0, n)
        marg_out[0, n] = marginal
        keep_marginal(0, n, marginal)
    for level in range(2, LEVELS):
        mask_factor(level)
    pl.semaphore_wait(barrier, cols_n + 1)
    ring(1, 0)
    pass_on(0, 0, 2)
    pass_on(0, 1, 2)

    def run(jobs):
        for job in jobs:
            if job[0] == "pass":
                forward(*job[1:])
            else:
                ring(*job)

    run(PREPARE)
    for level in range(1, LEVELS):
        run(BEFORE[level])
        for up in range(level - 1, -1, -1):
            receive(up, level - up)
        run(FIRST[level])
        if level < LEVELS - 1:
            ring_end(level, 0)
            ring_end(level, 1)
            select_and_cross(level, (0, 1))
        else:
            ring_end(level, 0)
            select_and_cross(level, (0,))
            run(BETWEEN)
            ring_end(level, 1)
            select_and_cross(level, (1,))
        run(MIDDLE[level])
        finish_level(level)
        run(AFTER[level])

    for level in range(1, LEVELS):
        ring_sent(level)
        for slab in (0,) if joint(level) else (0, 1):
            for copy in turn_all(level, slab):
                copy.wait_send()
    for level, k in SENDS:
        for copy in hop(level, k):
            copy.wait_send()


def solution(mesh):
    rows_n, cols_n = mesh.shape["row"], mesh.shape["col"]

    def shards(panel, diag_inverse, parents, sizes):
        pairs, per, lines, width = panel.shape
        vmem = pl.BlockSpec(memory_space=pltpu.VMEM)
        smem = pl.BlockSpec(memory_space=pltpu.SMEM)
        dma = pltpu.SemaphoreType.DMA

        def turn_shape(level):
            return (1 if joint(level) else 2, cols_n, lines, lanes_of(level))

        return pl.pallas_call(
            functools.partial(kernel, rows_n, cols_n),
            out_shape=(
                jax.ShapeDtypeStruct((pairs, per, lines, width), F32),
                jax.ShapeDtypeStruct((LEVELS, per, lines, width), F32),
            ),
            in_specs=[vmem, vmem, smem, smem],
            out_specs=(vmem, vmem),
            scratch_shapes=[
                *[pltpu.VMEM((2 * d, width, width), BF16) for d in range(1, 6)],
                *[pltpu.VMEM(turn_shape(d), BF16) for d in range(1, 6)],
                *[pltpu.VMEM(turn_shape(d), BF16) for d in range(1, 6)],
                *[pltpu.VMEM((per, 2 * level + 1, lines, width), BF16) for level, _ in HOPS],
                *[pltpu.VMEM((per, 3, 1, 128), F32) for _ in HOPS],
                pltpu.VMEM((320, 5 * width), BF16),
                pltpu.VMEM((cols_n, lines, 256), F32),
                pltpu.VMEM((4 * lines, width), F32),
                pltpu.VMEM((5, 2, 1, 128), F32),
                pltpu.VMEM((5, 2, cols_n, 1, 128), F32),
                dma((5,)),
                dma((5, 2, 4)),
                dma((5, 2)),
                dma((len(SENDS),)),
                dma((len(SENDS),)),
                dma((len(SENDS),)),
                dma((len(SENDS),)),
                dma((5, 2)),
                dma((5, 2)),
                dma((5, 2)),
                dma((5, 2)),
            ],
            compiler_params=pltpu.CompilerParams(
                collective_id=0, has_side_effects=True, vmem_limit_bytes=44000 * 1024
            ),
        )(panel, diag_inverse, parents, sizes)

    in_specs = (P(None, "row", "col", None), P(None, "row", "col", None), P(), P())
    out_specs = (P(None, "row", "col", None), P(None, "row", "col", None))
    return jax.shard_map(shards, mesh=mesh, in_specs=in_specs, out_specs=out_specs, check_vma=False)
```

```python
import functools

import jax
import jax.numpy as jnp
from jax import lax
from jax.experimental import pallas as pl
from jax.experimental.pallas import tpu as pltpu
from jax.sharding import PartitionSpec as P

MESH = pl.DeviceIdType.MESH
LEVELS = 6
F32 = jnp.float32
BF16 = jnp.bfloat16


POWER = 6
PREPARE = ((2, 0), (1, 1), (2, 1), (1, 2), (2, 2), (1, 3), (2, 3), (3, 0), (1, 4))
BEFORE = {1: (), 2: ((4, 1), (3, 3)), 3: ((4, 3), (5, 1, (0,))), 4: ((5, 1, (1,)), (5, 3, (0,))), 5: ()}
FIRST = {1: (('pass', 0, 1),), 2: (('pass', 1, 1), ('pass', 0, 4)), 3: (('pass', 2, 1),), 4: (('pass', 3, 1),), 5: ()}
BETWEEN = ((5, 4, (1,)),)
MIDDLE = {1: (('pass', 0, 2), (2, 4), (3, 1), (4, 0)), 2: (('pass', 1, 2), (4, 2), (3, 4)), 3: (('pass', 2, 2), (5, 0, (1,)), (4, 4)), 4: ((5, 2, (1,)), (5, 4, (0,))), 5: ()}
AFTER = {1: (('pass', 0, 3), (3, 2)), 2: (('pass', 1, 3), (5, 0, (0,))), 3: ((5, 2, (0,)),), 4: ((5, 3, (1,)),), 5: ()}
HOPS = tuple((level, k) for level in range(5) for k in range(6 - level))
SENDS = tuple((level, k) for level in range(5) for k in range(5 - level))


def joint(level):
    return level <= 2


def lanes_of(level):
    tall = 32 * level * (2 if joint(level) else 1)
    return 128 * (-(-tall // 128))


def scale_of(value):
    top = jnp.max(jnp.max(jnp.abs(value), axis=0, keepdims=True), axis=1, keepdims=True)
    return jnp.maximum(top, 1e-30).astype(BF16).astype(F32)


def encode(value, scale):
    unit = value * (1.0 / scale)
    square = unit * unit
    return unit * jnp.abs(unit) * (square * square)


def decode(code):
    root = jnp.exp(jnp.log(jnp.abs(code)) * (1.0 / POWER))
    return jnp.where(code > 0.0, root, jnp.where(code < 0.0, -root, 0.0))


def kernel(rows_n, cols_n, panel, diag, parents, sizes, cross_out, marg_out, *scratch):
    fulls = scratch[0:5]
    turn_out = scratch[5:10]
    turn_in = scratch[10:15]
    blocks = {place: scratch[15 + at] for at, place in enumerate(HOPS)}
    marks = {place: scratch[15 + len(HOPS) + at] for at, place in enumerate(HOPS)}
    (
        lhs, opened, turned_f32, mark_out, mark_in, factor_send, ring_recv, mate_recv,
        chain_send, chain_recv, scale_send, scale_recv, turn_send, turn_recv, mark_send, mark_recv,
    ) = scratch[15 + 2 * len(HOPS) :]
    width = diag.shape[3]
    lines = diag.shape[2]
    chips = cols_n // 2
    row = lax.axis_index("row")
    col = lax.axis_index("col")
    chip = col // 2
    core = col % 2
    mate = col + 1 - 2 * core
    right = (col + 2) % cols_n
    left = (col + cols_n - 2) % cols_n
    next_row = (row + 1) % rows_n
    prev_row = (row + rows_n - 1) % rows_n

    barrier = pltpu.get_barrier_semaphore()
    for peer in (right, left, mate):
        pl.semaphore_signal(barrier, inc=1, device_id=(row, peer), device_id_type=MESH)
    pl.semaphore_signal(barrier, inc=1, device_id=(next_row, col), device_id_type=MESH)
    pl.semaphore_signal(barrier, inc=1, device_id=(prev_row, col), device_id_type=MESH)
    line_of = lax.broadcasted_iota(jnp.int32, (lines, width), 0) + col * lines
    column_of = lax.broadcasted_iota(jnp.int32, (lines, width), 1)

    def base_of(level, n):
        size = sizes[level, row * 2 + n]
        live = (line_of < size) & (column_of < size)
        eye = (line_of == column_of) & (line_of >= size)
        return jnp.where(live, diag[level, n], jnp.where(eye, 1.0, 0.0))

    def strip(level, at, first, count):
        return fulls[level - 1].at[
            pl.ds(first, count), pl.ds(pl.multiple_of(at * lines, lines), lines), :
        ]

    def goes(n, way, step):
        return step < 3 or (step == 3 and way == n)

    def ring_copy(level, n, way, step):
        at = ((chip - step + chips) % chips if way == 0 else (chip + step) % chips) * 2 + core
        piece = strip(level, at, n * level, level)
        return pltpu.make_async_remote_copy(
            src_ref=piece, dst_ref=piece,
            send_sem=factor_send.at[level - 1],
            recv_sem=ring_recv.at[level - 1, n, step],
            device_id=(row, right if way == 0 else left), device_id_type=MESH,
        )

    def mate_copy(level, n, way, step):
        if step < 0:
            at = chip
        else:
            at = (chip - step - 1 + chips) % chips if way == 0 else (chip + step + 1) % chips
        piece = strip(level, at * 2 + core, n * level, level)
        return pltpu.make_async_remote_copy(
            src_ref=piece, dst_ref=piece,
            send_sem=factor_send.at[level - 1],
            recv_sem=mate_recv.at[level - 1, n],
            device_id=(row, mate), device_id_type=MESH,
        )

    def factor_wait(level, first, count, strips, send, recv):
        piece = fulls[level - 1].at[pl.ds(first, count), pl.ds(0, strips * lines), :]
        return pltpu.make_async_remote_copy(
            src_ref=piece, dst_ref=piece, send_sem=send, recv_sem=recv,
            device_id=(row, mate), device_id_type=MESH,
        )

    def mask_factor(level):
        start = level * (level - 1) // 2

        def one(n, _):
            node = row * 2 + n
            size = sizes[level, node]
            above = node
            for up in range(level - 1, -1, -1):
                above = parents[up, above]
                upper = sizes[up, above]
                keep = (line_of < upper) & (column_of < size)
                block = jnp.where(keep, panel[start + up, n].astype(F32), 0.0)
                fulls[level - 1][
                    n * level + up, pl.ds(pl.multiple_of(col * lines, lines), lines), :
                ] = block.astype(BF16)
            return 0

        lax.fori_loop(0, 2, one, 0)

    def ring(level, step, nodes=(0, 1)):
        for n in nodes:
            came = [way for way in (0, 1) if step > 0 and goes(n, way, step - 1)]
            if came:
                factor_wait(
                    level, n * level, level, len(came), factor_send.at[level - 1], ring_recv.at[level - 1, n, step - 1]
                ).wait_recv()
            for way in (0, 1):
                if goes(n, way, step):
                    ring_copy(level, n, way, step).start()
            if step == 0:
                mate_copy(level, n, 0, -1).start()
            for way in came:
                mate_copy(level, n, way, step - 1).start()

    def ring_end(level, n):
        factor_wait(
            level, n * level, level, 8, factor_send.at[level - 1], mate_recv.at[level - 1, n]
        ).wait_recv()

    def ring_sent(level):
        factor_wait(
            level, 0, 2 * level, 15, factor_send.at[level - 1], mate_recv.at[level - 1, 0]
        ).wait_send()

    def remote(src, dst, send, recv, place):
        return pltpu.make_async_remote_copy(
            src_ref=src, dst_ref=dst, send_sem=send, recv_sem=recv, device_id=place, device_id_type=MESH
        )

    def pass_on(level, n, part):
        place, at = (next_row, col), SENDS.index((level, 0))
        mark = pl.ds(0, 3) if level == 0 else pl.ds(part, 1)
        span = (pl.ds(0, level), pl.ds(level, level), pl.ds(2 * level, 1))[part]
        here, there = (level, 0), (level, 1)
        remote(
            marks[here].at[n, mark], marks[there].at[n, mark], scale_send.at[at], scale_recv.at[at], place
        ).start()
        remote(
            blocks[here].at[n, span], blocks[there].at[n, span], chain_send.at[at], chain_recv.at[at], place
        ).start()

    def hop(level, k):
        place, at = (next_row, col), SENDS.index((level, k))
        here, there = (level, k), (level, k + 1)
        return (
            remote(marks[here], marks[there], scale_send.at[at], scale_recv.at[at], place),
            remote(blocks[here], blocks[there], chain_send.at[at], chain_recv.at[at], place),
        )

    arrived = set()

    def receive(level, k):
        if (level, k) not in arrived:
            arrived.add((level, k))
            for copy in hop(level, k - 1):
                copy.wait_recv()

    def forward(level, k):
        receive(level, k)
        for copy in hop(level, k):
            copy.start()

    def turn_copies(level, slab, k):
        there = (col + k) % cols_n
        place = (row, there)
        return (
            remote(
                mark_out.at[level - 1, slab], mark_in.at[level - 1, slab, col],
                mark_send.at[level - 1, slab], mark_recv.at[level - 1, slab], place,
            ),
            remote(
                turn_out[level - 1].at[slab, there], turn_in[level - 1].at[slab, col],
                turn_send.at[level - 1, slab], turn_recv.at[level - 1, slab], place,
            ),
        )

    def turn_all(level, slab):
        most, place = pl.ds(0, cols_n - 1), (row, mate)
        marks = mark_in.at[level - 1, slab, most]
        pieces = turn_in[level - 1].at[slab, most]
        return (
            remote(marks, marks, mark_send.at[level - 1, slab], mark_recv.at[level - 1, slab], place),
            remote(pieces, pieces, turn_send.at[level - 1, slab], turn_recv.at[level - 1, slab], place),
        )

    def split(value):
        high = value.astype(BF16)
        return high, (value - high.astype(F32)).astype(BF16)

    lane_of = lax.broadcasted_iota(jnp.int32, (lines, 128), 1)
    per = 128 // lines
    sixteenth = lax.broadcasted_iota(jnp.int32, (16, 128), 0)

    def wide(scale):
        return jnp.concatenate([scale] * (width // 128), axis=1)

    def select_and_cross(level, nodes):
        start = level * (level - 1) // 2
        tall = lines * level

        def one(n, _):
            above = row * 2 + n
            within, distance = [None] * level, [None] * level
            for up in range(level - 1, -1, -1):
                above = parents[up, above]
                within[up] = lax.rem(above, 2)
                distance[up] = lax.rem(row + rows_n - lax.div(above, 2), rows_n)

            def pick(refs, up, entry):
                value = None
                for k in range(level - up + 1):
                    ref = refs[(up, k)]
                    there = ref[within[up]] if entry is None else ref[within[up], entry]
                    value = there if value is None else lax.select(distance[up] == k, there, value)
                return value

            table = [pick(marks, up, None) for up in range(level)]
            for l in range(level):
                for m in range(level):
                    up = max(l, m)
                    if l == m:
                        entry, which = 2 * up, 2
                    elif l < m:
                        entry, which = l, 0
                    else:
                        entry, which = up + m, 1
                    code = pick(blocks, up, entry)
                    high, low = split(decode(code.astype(F32)) * wide(table[up][which]))
                    lhs[l * lines : (l + 1) * lines, m * width : (m + 1) * width] = high
                    lhs[tall + l * lines : tall + (l + 1) * lines, m * width : (m + 1) * width] = low
            both = jnp.dot(
                lhs[0 : 2 * tall, 0 : level * width],
                fulls[level - 1][pl.ds(n * level, level)].reshape(level * width, width),
                preferred_element_type=F32,
            )
            crossed = -(both[0:tall, :] + both[tall : 2 * tall, :])
            scale = scale_of(crossed)
            code = encode(crossed, scale)
            for l in range(level):
                cross_out[start + l, n] = crossed[l * lines : (l + 1) * lines, :]
                if level < LEVELS - 1:
                    blocks[(level, 0)][n, l] = code[l * lines : (l + 1) * lines, :].astype(BF16)
            if level < LEVELS - 1:
                marks[(level, 0)][n, 0] = jnp.broadcast_to(scale, (1, 128))
                pass_on(level, n, 0)
            turned = jnp.transpose(code, (1, 0)).astype(BF16)
            slab = 0 if joint(level) else n
            first = n * tall if joint(level) else 0
            for c in range(cols_n):
                turn_out[level - 1][slab, c, :, first : first + tall] = turned[
                    c * lines : (c + 1) * lines, :
                ]
            lane = lax.broadcasted_iota(jnp.int32, (1, 128), 1)
            mark = jnp.broadcast_to(scale, (1, 128))
            if joint(level) and n == 1:
                mark = jnp.where(lane < tall, mark_out[level - 1, 0], mark)
            mark_out[level - 1, slab] = mark
            if not joint(level):
                send_turn(level, n)
            return 0

        if joint(level):
            one(0, 0)
            one(1, 0)
            send_turn(level, 0)
        elif len(nodes) == 1:
            one(nodes[0], 0)
        else:
            lax.fori_loop(0, 2, one, 0)

    def send_turn(level, slab):
        def send(k, _):
            for copy in turn_copies(level, slab, k):
                copy.start()
            return 0

        lax.fori_loop(1, cols_n, send, 0)
        turn_in[level - 1][slab, col] = turn_out[level - 1][slab, col]
        mark_in[level - 1, slab, col] = mark_out[level - 1, slab]

    def open_turn(level, slab):
        for copy in turn_all(level, slab):
            copy.wait_recv()
        lanes = lanes_of(level)

        def undo(c, _):
            code = turn_in[level - 1][slab, c].astype(F32)
            mark = jnp.concatenate([mark_in[level - 1, slab, c]] * (lanes // 128), axis=1)
            opened[c, :, 0:lanes] = decode(code) * mark
            return 0

        lax.fori_loop(0, cols_n, undo, 0)

    def finish_level(level):
        def one(n, _):
            if not joint(level):
                open_turn(level, n)
            for l in range(level):
                group = l + n * level if joint(level) else l
                for q in range(width // 128):
                    piece = None
                    for k in range(per):
                        source = opened[
                            q * per + k, :, (group // per) * 128 : (group // per) * 128 + 128
                        ]
                        shift = ((k - group % per) * lines) % 128
                        if shift:
                            source = pltpu.roll(source, shift, 1)
                        piece = source if piece is None else jnp.where(lane_of >= k * lines, source, piece)
                    high, low = split(piece)
                    lhs[0:lines, l * width + q * 128 : l * width + (q + 1) * 128] = high
                    lhs[lines : 2 * lines, l * width + q * 128 : l * width + (q + 1) * 128] = low
                    if level < LEVELS - 1:
                        turned_f32[l * lines : (l + 1) * lines, q * 128 : (q + 1) * 128] = piece
            if level < LEVELS - 1:
                whole = turned_f32[0 : level * lines, :]
                scale = scale_of(whole)
                code = encode(whole, scale).astype(BF16)
                for l in range(level):
                    blocks[(level, 0)][n, level + l] = code[l * lines : (l + 1) * lines, :]
                marks[(level, 0)][n, 1] = jnp.broadcast_to(scale, (1, 128))
                pass_on(level, n, 1)
            both = jnp.dot(
                lhs[0 : 2 * lines, 0 : level * width],
                fulls[level - 1][pl.ds(n * level, level)].reshape(level * width, width),
                preferred_element_type=F32,
            )
            marginal = base_of(level, n) - (both[0:lines, :] + both[lines : 2 * lines, :])
            marg_out[level, n] = marginal
            if level < LEVELS - 1:
                send_marginal(level, n, marginal)
            return 0

        if joint(level):
            open_turn(level, 0)
            one(0, 0)
            one(1, 0)
        else:
            lax.fori_loop(0, 2, one, 0)

    def keep_marginal(level, n, marginal):
        scale = scale_of(marginal)
        blocks[(level, 0)][n, 2 * level] = encode(marginal, scale).astype(BF16)
        for entry in range(3) if level == 0 else (2,):
            marks[(level, 0)][n, entry] = jnp.broadcast_to(scale, (1, 128))

    def send_marginal(level, n, marginal):
        keep_marginal(level, n, marginal)
        pass_on(level, n, 2)

    mask_factor(1)
    for n in range(2):
        marginal = base_of(0, n)
        marg_out[0, n] = marginal
        keep_marginal(0, n, marginal)
    for level in range(2, LEVELS):
        mask_factor(level)
    pl.semaphore_wait(barrier, 5)
    ring(1, 0)
    pass_on(0, 0, 2)
    pass_on(0, 1, 2)

    def run(jobs):
        for job in jobs:
            if job[0] == "pass":
                forward(*job[1:])
            else:
                ring(*job)

    run(PREPARE)
    for level in range(1, LEVELS):
        run(BEFORE[level])
        for up in range(level - 1, -1, -1):
            receive(up, level - up)
        run(FIRST[level])
        if level < LEVELS - 1:
            ring_end(level, 0)
            ring_end(level, 1)
            select_and_cross(level, (0, 1))
        else:
            ring_end(level, 0)
            select_and_cross(level, (0,))
            run(BETWEEN)
            ring_end(level, 1)
            select_and_cross(level, (1,))
        run(MIDDLE[level])
        finish_level(level)
        run(AFTER[level])

    for level in range(1, LEVELS):
        ring_sent(level)
        for slab in (0,) if joint(level) else (0, 1):
            for copy in turn_all(level, slab):
                copy.wait_send()
    for level, k in SENDS:
        for copy in hop(level, k):
            copy.wait_send()


def solution(mesh):
    rows_n, cols_n = mesh.shape["row"], mesh.shape["col"]

    def shards(panel, diag_inverse, parents, sizes):
        pairs, per, lines, width = panel.shape
        vmem = pl.BlockSpec(memory_space=pltpu.VMEM)
        smem = pl.BlockSpec(memory_space=pltpu.SMEM)
        dma = pltpu.SemaphoreType.DMA

        def turn_shape(level):
            return (1 if joint(level) else 2, cols_n, lines, lanes_of(level))

        return pl.pallas_call(
            functools.partial(kernel, rows_n, cols_n),
            out_shape=(
                jax.ShapeDtypeStruct((pairs, per, lines, width), F32),
                jax.ShapeDtypeStruct((LEVELS, per, lines, width), F32),
            ),
            in_specs=[vmem, vmem, smem, smem],
            out_specs=(vmem, vmem),
            scratch_shapes=[
                *[pltpu.VMEM((2 * d, width, width), BF16) for d in range(1, 6)],
                *[pltpu.VMEM(turn_shape(d), BF16) for d in range(1, 6)],
                *[pltpu.VMEM(turn_shape(d), BF16) for d in range(1, 6)],
                *[pltpu.VMEM((per, 2 * level + 1, lines, width), BF16) for level, _ in HOPS],
                *[pltpu.VMEM((per, 3, 1, 128), F32) for _ in HOPS],
                pltpu.VMEM((320, 5 * width), BF16),
                pltpu.VMEM((cols_n, lines, 256), F32),
                pltpu.VMEM((4 * lines, width), F32),
                pltpu.VMEM((5, 2, 1, 128), F32),
                pltpu.VMEM((5, 2, cols_n, 1, 128), F32),
                dma((5,)),
                dma((5, 2, 4)),
                dma((5, 2)),
                dma((len(SENDS),)),
                dma((len(SENDS),)),
                dma((len(SENDS),)),
                dma((len(SENDS),)),
                dma((5, 2)),
                dma((5, 2)),
                dma((5, 2)),
                dma((5, 2)),
            ],
            compiler_params=pltpu.CompilerParams(
                collective_id=0, has_side_effects=True, vmem_limit_bytes=44000 * 1024
            ),
        )(panel, diag_inverse, parents, sizes)

    in_specs = (P(None, "row", "col", None), P(None, "row", "col", None), P(), P())
    out_specs = (P(None, "row", "col", None), P(None, "row", "col", None))
    return jax.shard_map(shards, mesh=mesh, in_specs=in_specs, out_specs=out_specs, check_vma=False)
```

```python
import functools

import jax
import jax.numpy as jnp
from jax import lax
from jax.experimental import pallas as pl
from jax.experimental.pallas import tpu as pltpu
from jax.sharding import PartitionSpec as P

MESH = pl.DeviceIdType.MESH
LEVELS = 6
F32 = jnp.float32
BF16 = jnp.bfloat16


POWER = 6
PREPARE = ((2, 0), (1, 1), (2, 1), (1, 2), (2, 2), (1, 3), (2, 3), (3, 0), (1, 4))
BEFORE = {1: (), 2: ((4, 1), (3, 3)), 3: ((4, 3), (5, 1, (0,))), 4: ((5, 1, (1,)), (5, 3, (0,))), 5: ()}
FIRST = {1: (('pass', 0, 1),), 2: (('pass', 1, 1), ('pass', 0, 4)), 3: (('pass', 2, 1),), 4: (('pass', 3, 1),), 5: ()}
BETWEEN = ((5, 4, (1,)),)
MIDDLE = {1: (('pass', 0, 2), (2, 4), (3, 1), (4, 0)), 2: (('pass', 1, 2), (4, 2), (3, 4)), 3: (('pass', 2, 2), (5, 0, (1,)), (4, 4)), 4: ((5, 2, (1,)), (5, 4, (0,))), 5: ()}
AFTER = {1: (('pass', 0, 3), (3, 2)), 2: (('pass', 1, 3), (5, 0, (0,))), 3: ((5, 2, (0,)),), 4: ((5, 3, (1,)),), 5: ()}
HOPS = tuple((level, k) for level in range(5) for k in range(6 - level))
SENDS = tuple((level, k) for level in range(5) for k in range(5 - level))


def joint(level):
    return level <= 2


def slabs_of(level):
    return 1 if joint(level) else 2 if level < 5 else 3


def scale_of(value):
    top = jnp.max(jnp.max(jnp.abs(value), axis=0, keepdims=True), axis=1, keepdims=True)
    return jnp.maximum(top, 1e-30).astype(BF16).astype(F32)


def encode(value, scale):
    unit = value * (1.0 / scale)
    square = unit * unit
    return unit * jnp.abs(unit) * (square * square)


def decode(code):
    root = jnp.exp(jnp.log(jnp.abs(code)) * (1.0 / POWER))
    return jnp.where(code > 0.0, root, jnp.where(code < 0.0, -root, 0.0))


def kernel(rows_n, cols_n, panel, diag, parents, sizes, cross_out, marg_out, *scratch):
    fulls = scratch[0:5]
    turn_out = scratch[5:10]
    turn_in = scratch[10:15]
    blocks = {place: scratch[15 + at] for at, place in enumerate(HOPS)}
    marks = {place: scratch[15 + len(HOPS) + at] for at, place in enumerate(HOPS)}
    (
        lhs, opened, turned_f32, mark_out, mark_in, factor_send, ring_recv, mate_recv,
        chain_send, chain_recv, scale_send, scale_recv, turn_send, turn_recv, mark_send, mark_recv,
    ) = scratch[15 + 2 * len(HOPS) :]
    width = diag.shape[3]
    lines = diag.shape[2]
    chips = cols_n // 2
    row = lax.axis_index("row")
    col = lax.axis_index("col")
    chip = col // 2
    core = col % 2
    mate = col + 1 - 2 * core
    right = (col + 2) % cols_n
    left = (col + cols_n - 2) % cols_n
    next_row = (row + 1) % rows_n
    prev_row = (row + rows_n - 1) % rows_n

    barrier = pltpu.get_barrier_semaphore()
    for peer in (right, left, mate):
        pl.semaphore_signal(barrier, inc=1, device_id=(row, peer), device_id_type=MESH)
    pl.semaphore_signal(barrier, inc=1, device_id=(next_row, col), device_id_type=MESH)
    pl.semaphore_signal(barrier, inc=1, device_id=(prev_row, col), device_id_type=MESH)
    line_of = lax.broadcasted_iota(jnp.int32, (lines, width), 0) + col * lines
    column_of = lax.broadcasted_iota(jnp.int32, (lines, width), 1)

    def base_of(level, n):
        size = sizes[level, row * 2 + n]
        live = (line_of < size) & (column_of < size)
        eye = (line_of == column_of) & (line_of >= size)
        return jnp.where(live, diag[level, n], jnp.where(eye, 1.0, 0.0))

    def strip(level, at, first, count):
        return fulls[level - 1].at[
            pl.ds(first, count), pl.ds(pl.multiple_of(at * lines, lines), lines), :
        ]

    def goes(n, way, step):
        return step < 3 or (step == 3 and way == n)

    def ring_copy(level, n, way, step):
        at = ((chip - step + chips) % chips if way == 0 else (chip + step) % chips) * 2 + core
        piece = strip(level, at, n * level, level)
        return pltpu.make_async_remote_copy(
            src_ref=piece, dst_ref=piece,
            send_sem=factor_send.at[level - 1],
            recv_sem=ring_recv.at[level - 1, n, step],
            device_id=(row, right if way == 0 else left), device_id_type=MESH,
        )

    def mate_copy(level, n, way, step):
        if step < 0:
            at = chip
        else:
            at = (chip - step - 1 + chips) % chips if way == 0 else (chip + step + 1) % chips
        piece = strip(level, at * 2 + core, n * level, level)
        return pltpu.make_async_remote_copy(
            src_ref=piece, dst_ref=piece,
            send_sem=factor_send.at[level - 1],
            recv_sem=mate_recv.at[level - 1, n],
            device_id=(row, mate), device_id_type=MESH,
        )

    def factor_wait(level, first, count, strips, send, recv):
        piece = fulls[level - 1].at[pl.ds(first, count), pl.ds(0, strips * lines), :]
        return pltpu.make_async_remote_copy(
            src_ref=piece, dst_ref=piece, send_sem=send, recv_sem=recv,
            device_id=(row, mate), device_id_type=MESH,
        )

    def mask_factor(level):
        start = level * (level - 1) // 2

        def one(n, _):
            node = row * 2 + n
            size = sizes[level, node]
            above = node
            for up in range(level - 1, -1, -1):
                above = parents[up, above]
                upper = sizes[up, above]
                keep = (line_of < upper) & (column_of < size)
                block = jnp.where(keep, panel[start + up, n].astype(F32), 0.0)
                fulls[level - 1][
                    n * level + up, pl.ds(pl.multiple_of(col * lines, lines), lines), :
                ] = block.astype(BF16)
            return 0

        lax.fori_loop(0, 2, one, 0)

    def ring(level, step, nodes=(0, 1)):
        for n in nodes:
            came = [way for way in (0, 1) if step > 0 and goes(n, way, step - 1)]
            if came:
                factor_wait(
                    level, n * level, level, len(came), factor_send.at[level - 1], ring_recv.at[level - 1, n, step - 1]
                ).wait_recv()
            for way in (0, 1):
                if goes(n, way, step):
                    ring_copy(level, n, way, step).start()
            if step == 0:
                mate_copy(level, n, 0, -1).start()
            for way in came:
                mate_copy(level, n, way, step - 1).start()

    def ring_end(level, n):
        factor_wait(
            level, n * level, level, 8, factor_send.at[level - 1], mate_recv.at[level - 1, n]
        ).wait_recv()

    def ring_sent(level):
        factor_wait(
            level, 0, 2 * level, 15, factor_send.at[level - 1], mate_recv.at[level - 1, 0]
        ).wait_send()

    def remote(src, dst, send, recv, place):
        return pltpu.make_async_remote_copy(
            src_ref=src, dst_ref=dst, send_sem=send, recv_sem=recv, device_id=place, device_id_type=MESH
        )

    def pass_on(level, n, part):
        place, at = (next_row, col), SENDS.index((level, 0))
        mark = pl.ds(0, 3) if level == 0 else pl.ds(part, 1)
        span = (pl.ds(0, level), pl.ds(level, level), pl.ds(2 * level, 1))[part]
        here, there = (level, 0), (level, 1)
        remote(
            marks[here].at[n, mark], marks[there].at[n, mark], scale_send.at[at], scale_recv.at[at], place
        ).start()
        remote(
            blocks[here].at[n, span], blocks[there].at[n, span], chain_send.at[at], chain_recv.at[at], place
        ).start()

    def hop(level, k):
        place, at = (next_row, col), SENDS.index((level, k))
        here, there = (level, k), (level, k + 1)
        return (
            remote(marks[here], marks[there], scale_send.at[at], scale_recv.at[at], place),
            remote(blocks[here], blocks[there], chain_send.at[at], chain_recv.at[at], place),
        )

    arrived = set()

    def receive(level, k):
        if (level, k) not in arrived:
            arrived.add((level, k))
            for copy in hop(level, k - 1):
                copy.wait_recv()

    def forward(level, k):
        receive(level, k)
        for copy in hop(level, k):
            copy.start()

    def turn_copies(level, slab, k):
        there = (col + k) % cols_n
        place = (row, there)
        return (
            remote(
                mark_out.at[level - 1, slab], mark_in.at[level - 1, slab, col],
                mark_send.at[level - 1, slab], mark_recv.at[level - 1, slab], place,
            ),
            remote(
                turn_out[level - 1].at[slab, there], turn_in[level - 1].at[slab, col],
                turn_send.at[level - 1, slab], turn_recv.at[level - 1, slab], place,
            ),
        )

    def turn_all(level, slab):
        most, place = pl.ds(0, cols_n - 1), (row, mate)
        marks = mark_in.at[level - 1, slab, most]
        pieces = turn_in[level - 1].at[slab, most]
        return (
            remote(marks, marks, mark_send.at[level - 1, slab], mark_recv.at[level - 1, slab], place),
            remote(pieces, pieces, turn_send.at[level - 1, slab], turn_recv.at[level - 1, slab], place),
        )

    def split(value):
        high = value.astype(BF16)
        return high, (value - high.astype(F32)).astype(BF16)

    lane_of = lax.broadcasted_iota(jnp.int32, (lines, 128), 1)
    per = 128 // lines
    sixteenth = lax.broadcasted_iota(jnp.int32, (16, 128), 0)

    def wide(scale):
        return jnp.concatenate([scale] * (width // 128), axis=1)

    def select_and_cross(level, nodes):
        start = level * (level - 1) // 2
        tall = lines * level

        def one(n, _):
            above = row * 2 + n
            within, distance = [None] * level, [None] * level
            for up in range(level - 1, -1, -1):
                above = parents[up, above]
                within[up] = lax.rem(above, 2)
                distance[up] = lax.rem(row + rows_n - lax.div(above, 2), rows_n)

            def pick(refs, up, entry):
                value = None
                for k in range(level - up + 1):
                    ref = refs[(up, k)]
                    there = ref[within[up]] if entry is None else ref[within[up], entry]
                    value = there if value is None else lax.select(distance[up] == k, there, value)
                return value

            table = [pick(marks, up, None) for up in range(level)]
            for l in range(level):
                for m in range(level):
                    up = max(l, m)
                    if l == m:
                        entry, which = 2 * up, 2
                    elif l < m:
                        entry, which = l, 0
                    else:
                        entry, which = up + m, 1
                    code = pick(blocks, up, entry)
                    high, low = split(decode(code.astype(F32)) * wide(table[up][which]))
                    lhs[l * lines : (l + 1) * lines, m * width : (m + 1) * width] = high
                    lhs[tall + l * lines : tall + (l + 1) * lines, m * width : (m + 1) * width] = low
            both = jnp.dot(
                lhs[0 : 2 * tall, 0 : level * width],
                fulls[level - 1][pl.ds(n * level, level)].reshape(level * width, width),
                preferred_element_type=F32,
            )
            crossed = -(both[0:tall, :] + both[tall : 2 * tall, :])
            scale = scale_of(crossed)
            code = encode(crossed, scale)
            for l in range(level):
                cross_out[start + l, n] = crossed[l * lines : (l + 1) * lines, :]
                if level < LEVELS - 1:
                    blocks[(level, 0)][n, l] = code[l * lines : (l + 1) * lines, :].astype(BF16)
            if level < LEVELS - 1:
                marks[(level, 0)][n, 0] = jnp.broadcast_to(scale, (1, 128))
                pass_on(level, n, 0)
            turned = jnp.transpose(code, (1, 0)).astype(BF16)
            slab = 0 if joint(level) else n
            first = n * tall if joint(level) else 0
            for c in range(cols_n):
                piece = turned[c * lines : (c + 1) * lines, :]
                turn_out[level - 1][slab, c, :, first : first + min(tall, 128)] = piece[:, 0:128]
                if tall > 128:
                    turn_out[level - 1][2, c, :, n * lines : (n + 1) * lines] = piece[:, 128:tall]
            lane = lax.broadcasted_iota(jnp.int32, (1, 128), 1)
            mark = jnp.broadcast_to(scale, (1, 128))
            if joint(level) and n == 1:
                mark = jnp.where(lane < tall, mark_out[level - 1, 0], mark)
            mark_out[level - 1, slab] = mark
            if tall > 128:
                if n == 1:
                    mark = jnp.where(lane < lines, mark_out[level - 1, 2], mark)
                mark_out[level - 1, 2] = mark
                if n == 1:
                    send_turn(level, 2)
            if not joint(level):
                send_turn(level, n)
            return 0

        if joint(level):
            one(0, 0)
            one(1, 0)
            send_turn(level, 0)
        elif len(nodes) == 1:
            one(nodes[0], 0)
        else:
            lax.fori_loop(0, 2, one, 0)

    def send_turn(level, slab):
        def send(k, _):
            for copy in turn_copies(level, slab, k):
                copy.start()
            return 0

        lax.fori_loop(1, cols_n, send, 0)
        turn_in[level - 1][slab, col] = turn_out[level - 1][slab, col]
        mark_in[level - 1, slab, col] = mark_out[level - 1, slab]

    def open_turn(level, slab):
        for copy in turn_all(level, slab):
            copy.wait_recv()
        place = 128 if slabs_of(level) == 3 and slab == 2 else 0

        def undo(c, _):
            code = turn_in[level - 1][slab, c].astype(F32)
            opened[c, :, place : place + 128] = decode(code) * mark_in[level - 1, slab, c]
            return 0

        lax.fori_loop(0, cols_n, undo, 0)

    def finish_level(level):
        def one(n, _):
            if not joint(level):
                if slabs_of(level) == 3 and n == 0:
                    open_turn(level, 2)
                open_turn(level, n)
            for l in range(level):
                group = l + n * level if joint(level) else l if l < 4 else 4 + n
                for q in range(width // 128):
                    piece = None
                    for k in range(per):
                        source = opened[
                            q * per + k, :, (group // per) * 128 : (group // per) * 128 + 128
                        ]
                        shift = ((k - group % per) * lines) % 128
                        if shift:
                            source = pltpu.roll(source, shift, 1)
                        piece = source if piece is None else jnp.where(lane_of >= k * lines, source, piece)
                    high, low = split(piece)
                    lhs[0:lines, l * width + q * 128 : l * width + (q + 1) * 128] = high
                    lhs[lines : 2 * lines, l * width + q * 128 : l * width + (q + 1) * 128] = low
                    if level < LEVELS - 1:
                        turned_f32[l * lines : (l + 1) * lines, q * 128 : (q + 1) * 128] = piece
            if level < LEVELS - 1:
                whole = turned_f32[0 : level * lines, :]
                scale = scale_of(whole)
                code = encode(whole, scale).astype(BF16)
                for l in range(level):
                    blocks[(level, 0)][n, level + l] = code[l * lines : (l + 1) * lines, :]
                marks[(level, 0)][n, 1] = jnp.broadcast_to(scale, (1, 128))
                pass_on(level, n, 1)
            both = jnp.dot(
                lhs[0 : 2 * lines, 0 : level * width],
                fulls[level - 1][pl.ds(n * level, level)].reshape(level * width, width),
                preferred_element_type=F32,
            )
            marginal = base_of(level, n) - (both[0:lines, :] + both[lines : 2 * lines, :])
            marg_out[level, n] = marginal
            if level < LEVELS - 1:
                send_marginal(level, n, marginal)
            return 0

        if joint(level):
            open_turn(level, 0)
            one(0, 0)
            one(1, 0)
        elif slabs_of(level) == 2:
            lax.fori_loop(0, 2, one, 0)
        else:
            one(0, 0)
            one(1, 0)

    def keep_marginal(level, n, marginal):
        scale = scale_of(marginal)
        blocks[(level, 0)][n, 2 * level] = encode(marginal, scale).astype(BF16)
        for entry in range(3) if level == 0 else (2,):
            marks[(level, 0)][n, entry] = jnp.broadcast_to(scale, (1, 128))

    def send_marginal(level, n, marginal):
        keep_marginal(level, n, marginal)
        pass_on(level, n, 2)

    mask_factor(1)
    for n in range(2):
        marginal = base_of(0, n)
        marg_out[0, n] = marginal
        keep_marginal(0, n, marginal)
    for level in range(2, LEVELS):
        mask_factor(level)
    pl.semaphore_wait(barrier, 5)
    ring(1, 0)
    pass_on(0, 0, 2)
    pass_on(0, 1, 2)

    def run(jobs):
        for job in jobs:
            if job[0] == "pass":
                forward(*job[1:])
            else:
                ring(*job)

    run(PREPARE)
    for level in range(1, LEVELS):
        run(BEFORE[level])
        for up in range(level - 1, -1, -1):
            receive(up, level - up)
        run(FIRST[level])
        if level < LEVELS - 1:
            ring_end(level, 0)
            ring_end(level, 1)
            select_and_cross(level, (0, 1))
        else:
            ring_end(level, 0)
            select_and_cross(level, (0,))
            run(BETWEEN)
            ring_end(level, 1)
            select_and_cross(level, (1,))
        run(MIDDLE[level])
        finish_level(level)
        run(AFTER[level])

    for level in range(1, LEVELS):
        ring_sent(level)
        for slab in range(slabs_of(level)):
            for copy in turn_all(level, slab):
                copy.wait_send()
    for level, k in SENDS:
        for copy in hop(level, k):
            copy.wait_send()


def solution(mesh):
    rows_n, cols_n = mesh.shape["row"], mesh.shape["col"]

    def shards(panel, diag_inverse, parents, sizes):
        pairs, per, lines, width = panel.shape
        vmem = pl.BlockSpec(memory_space=pltpu.VMEM)
        smem = pl.BlockSpec(memory_space=pltpu.SMEM)
        dma = pltpu.SemaphoreType.DMA

        def turn_shape(level):
            return (slabs_of(level), cols_n, lines, 128)

        return pl.pallas_call(
            functools.partial(kernel, rows_n, cols_n),
            out_shape=(
                jax.ShapeDtypeStruct((pairs, per, lines, width), F32),
                jax.ShapeDtypeStruct((LEVELS, per, lines, width), F32),
            ),
            in_specs=[vmem, vmem, smem, smem],
            out_specs=(vmem, vmem),
            scratch_shapes=[
                *[pltpu.VMEM((2 * d, width, width), BF16) for d in range(1, 6)],
                *[pltpu.VMEM(turn_shape(d), BF16) for d in range(1, 6)],
                *[pltpu.VMEM(turn_shape(d), BF16) for d in range(1, 6)],
                *[pltpu.VMEM((per, 2 * level + 1, lines, width), BF16) for level, _ in HOPS],
                *[pltpu.VMEM((per, 3, 1, 128), F32) for _ in HOPS],
                pltpu.VMEM((320, 5 * width), BF16),
                pltpu.VMEM((cols_n, lines, 256), F32),
                pltpu.VMEM((4 * lines, width), F32),
                pltpu.VMEM((5, 3, 1, 128), F32),
                pltpu.VMEM((5, 3, cols_n, 1, 128), F32),
                dma((5,)),
                dma((5, 2, 4)),
                dma((5, 2)),
                dma((len(SENDS),)),
                dma((len(SENDS),)),
                dma((len(SENDS),)),
                dma((len(SENDS),)),
                dma((5, 3)),
                dma((5, 3)),
                dma((5, 3)),
                dma((5, 3)),
            ],
            compiler_params=pltpu.CompilerParams(
                collective_id=0, has_side_effects=True, vmem_limit_bytes=44000 * 1024
            ),
        )(panel, diag_inverse, parents, sizes)

    in_specs = (P(None, "row", "col", None), P(None, "row", "col", None), P(), P())
    out_specs = (P(None, "row", "col", None), P(None, "row", "col", None))
    return jax.shard_map(shards, mesh=mesh, in_specs=in_specs, out_specs=out_specs, check_vma=False)
```

```python
import functools

import jax
import jax.numpy as jnp
from jax import lax
from jax.experimental import pallas as pl
from jax.experimental.pallas import tpu as pltpu
from jax.sharding import PartitionSpec as P

MESH = pl.DeviceIdType.MESH
LEVELS = 6
F32 = jnp.float32
BF16 = jnp.bfloat16


POWER = 6
PREPARE = ((2, 0), (1, 1), (2, 1), (1, 2), (2, 2), (1, 3), (1, 4))
BEFORE = {1: (), 2: ((3, 2),), 3: ((4, 2),), 4: (), 5: ()}
FIRST = {1: (('pass', 0, 1),), 2: (('pass', 1, 1), ('pass', 0, 4)), 3: (('pass', 2, 1),), 4: (('pass', 3, 1),), 5: ()}
BETWEEN = ((5, 4, (1,)),)
MIDDLE = {1: (('pass', 0, 2), (2, 3), (3, 0)), 2: (('pass', 1, 2), (3, 3), (4, 0)), 3: (('pass', 2, 2), (4, 3), (5, 0, (0,))), 4: ((5, 2, (0,)), (5, 1, (1,)), (5, 3, (0,))), 5: ()}
AFTER = {1: (('pass', 0, 3), (2, 4), (3, 1)), 2: (('pass', 1, 3), (3, 4), (4, 1)), 3: ((4, 4), (5, 1, (0,)), (5, 0, (1,))), 4: ((5, 2, (1,)), (5, 4, (0,)), (5, 3, (1,))), 5: ()}
HOPS = tuple((level, k) for level in range(5) for k in range(6 - level))
SENDS = tuple((level, k) for level in range(5) for k in range(5 - level))


def joint(level):
    return level <= 2


def slabs_of(level):
    return 1 if joint(level) else 2 if level < 5 else 3


def scale_of(value):
    top = jnp.max(jnp.max(jnp.abs(value), axis=0, keepdims=True), axis=1, keepdims=True)
    return jnp.maximum(top, 1e-30).astype(BF16).astype(F32)


def encode(value, scale):
    unit = value * (1.0 / scale)
    square = unit * unit
    return unit * jnp.abs(unit) * (square * square)


def decode(code):
    root = jnp.exp(jnp.log(jnp.abs(code)) * (1.0 / POWER))
    return jnp.where(code > 0.0, root, jnp.where(code < 0.0, -root, 0.0))


def kernel(rows_n, cols_n, panel, diag, parents, sizes, cross_out, marg_out, *scratch):
    fulls = scratch[0:5]
    turn_out = scratch[5:10]
    turn_in = scratch[10:15]
    blocks = {place: scratch[15 + at] for at, place in enumerate(HOPS)}
    marks = {place: scratch[15 + len(HOPS) + at] for at, place in enumerate(HOPS)}
    (
        lhs, opened, turned_f32, mark_out, mark_in, factor_send, ring_recv, mate_recv,
        chain_send, chain_recv, scale_send, scale_recv, turn_send, turn_recv, mark_send, mark_recv,
    ) = scratch[15 + 2 * len(HOPS) :]
    width = diag.shape[3]
    lines = diag.shape[2]
    chips = cols_n // 2
    row = lax.axis_index("row")
    col = lax.axis_index("col")
    chip = col // 2
    core = col % 2
    mate = col + 1 - 2 * core
    right = (col + 2) % cols_n
    left = (col + cols_n - 2) % cols_n
    next_row = (row + 1) % rows_n
    prev_row = (row + rows_n - 1) % rows_n

    barrier = pltpu.get_barrier_semaphore()
    for peer in (right, left, mate):
        pl.semaphore_signal(barrier, inc=1, device_id=(row, peer), device_id_type=MESH)
    pl.semaphore_signal(barrier, inc=1, device_id=(next_row, col), device_id_type=MESH)
    pl.semaphore_signal(barrier, inc=1, device_id=(prev_row, col), device_id_type=MESH)
    line_of = lax.broadcasted_iota(jnp.int32, (lines, width), 0) + col * lines
    column_of = lax.broadcasted_iota(jnp.int32, (lines, width), 1)

    def base_of(level, n):
        size = sizes[level, row * 2 + n]
        live = (line_of < size) & (column_of < size)
        eye = (line_of == column_of) & (line_of >= size)
        return jnp.where(live, diag[level, n], jnp.where(eye, 1.0, 0.0))

    def strip(level, at, first, count):
        return fulls[level - 1].at[
            pl.ds(first, count), pl.ds(pl.multiple_of(at * lines, lines), lines), :
        ]

    def goes(n, way, step):
        return step < 3 or (step == 3 and way == n)

    def ring_copy(level, n, way, step):
        at = ((chip - step + chips) % chips if way == 0 else (chip + step) % chips) * 2 + core
        piece = strip(level, at, n * level, level)
        return pltpu.make_async_remote_copy(
            src_ref=piece, dst_ref=piece,
            send_sem=factor_send.at[level - 1],
            recv_sem=ring_recv.at[level - 1, n, step],
            device_id=(row, right if way == 0 else left), device_id_type=MESH,
        )

    def mate_copy(level, n, way, step):
        if step < 0:
            at = chip
        else:
            at = (chip - step - 1 + chips) % chips if way == 0 else (chip + step + 1) % chips
        piece = strip(level, at * 2 + core, n * level, level)
        return pltpu.make_async_remote_copy(
            src_ref=piece, dst_ref=piece,
            send_sem=factor_send.at[level - 1],
            recv_sem=mate_recv.at[level - 1, n],
            device_id=(row, mate), device_id_type=MESH,
        )

    def factor_wait(level, first, count, strips, send, recv):
        piece = fulls[level - 1].at[pl.ds(first, count), pl.ds(0, strips * lines), :]
        return pltpu.make_async_remote_copy(
            src_ref=piece, dst_ref=piece, send_sem=send, recv_sem=recv,
            device_id=(row, mate), device_id_type=MESH,
        )

    def mask_factor(level):
        start = level * (level - 1) // 2

        def one(n, _):
            node = row * 2 + n
            size = sizes[level, node]
            above = node
            for up in range(level - 1, -1, -1):
                above = parents[up, above]
                upper = sizes[up, above]
                keep = (line_of < upper) & (column_of < size)
                block = jnp.where(keep, panel[start + up, n].astype(F32), 0.0)
                fulls[level - 1][
                    n * level + up, pl.ds(pl.multiple_of(col * lines, lines), lines), :
                ] = block.astype(BF16)
            return 0

        lax.fori_loop(0, 2, one, 0)

    def ring(level, step, nodes=(0, 1)):
        for n in nodes:
            came = [way for way in (0, 1) if step > 0 and goes(n, way, step - 1)]
            if came:
                factor_wait(
                    level, n * level, level, len(came), factor_send.at[level - 1], ring_recv.at[level - 1, n, step - 1]
                ).wait_recv()
            for way in (0, 1):
                if goes(n, way, step):
                    ring_copy(level, n, way, step).start()
            if step == 0:
                mate_copy(level, n, 0, -1).start()
            for way in came:
                mate_copy(level, n, way, step - 1).start()

    def ring_end(level, n):
        factor_wait(
            level, n * level, level, 8, factor_send.at[level - 1], mate_recv.at[level - 1, n]
        ).wait_recv()

    def ring_sent(level):
        factor_wait(
            level, 0, 2 * level, 15, factor_send.at[level - 1], mate_recv.at[level - 1, 0]
        ).wait_send()

    def remote(src, dst, send, recv, place):
        return pltpu.make_async_remote_copy(
            src_ref=src, dst_ref=dst, send_sem=send, recv_sem=recv, device_id=place, device_id_type=MESH
        )

    def pass_on(level, n, part):
        place, at = (next_row, col), SENDS.index((level, 0))
        mark = pl.ds(0, 3) if level == 0 else pl.ds(part, 1)
        span = (pl.ds(0, level), pl.ds(level, level), pl.ds(2 * level, 1))[part]
        here, there = (level, 0), (level, 1)
        remote(
            marks[here].at[n, mark], marks[there].at[n, mark], scale_send.at[at], scale_recv.at[at], place
        ).start()
        remote(
            blocks[here].at[n, span], blocks[there].at[n, span], chain_send.at[at], chain_recv.at[at], place
        ).start()

    def hop(level, k):
        place, at = (next_row, col), SENDS.index((level, k))
        here, there = (level, k), (level, k + 1)
        return (
            remote(marks[here], marks[there], scale_send.at[at], scale_recv.at[at], place),
            remote(blocks[here], blocks[there], chain_send.at[at], chain_recv.at[at], place),
        )

    arrived = set()

    def receive(level, k):
        if (level, k) not in arrived:
            arrived.add((level, k))
            for copy in hop(level, k - 1):
                copy.wait_recv()

    def forward(level, k):
        receive(level, k)
        for copy in hop(level, k):
            copy.start()

    def turn_copies(level, slab, k):
        there = (col + k) % cols_n
        place = (row, there)
        return (
            remote(
                mark_out.at[level - 1, slab], mark_in.at[level - 1, slab, col],
                mark_send.at[level - 1, slab], mark_recv.at[level - 1, slab], place,
            ),
            remote(
                turn_out[level - 1].at[slab, there], turn_in[level - 1].at[slab, col],
                turn_send.at[level - 1, slab], turn_recv.at[level - 1, slab], place,
            ),
        )

    def turn_all(level, slab):
        most, place = pl.ds(0, cols_n - 1), (row, mate)
        marks = mark_in.at[level - 1, slab, most]
        pieces = turn_in[level - 1].at[slab, most]
        return (
            remote(marks, marks, mark_send.at[level - 1, slab], mark_recv.at[level - 1, slab], place),
            remote(pieces, pieces, turn_send.at[level - 1, slab], turn_recv.at[level - 1, slab], place),
        )

    def split(value):
        high = value.astype(BF16)
        return high, (value - high.astype(F32)).astype(BF16)

    lane_of = lax.broadcasted_iota(jnp.int32, (lines, 128), 1)
    per = 128 // lines
    sixteenth = lax.broadcasted_iota(jnp.int32, (16, 128), 0)

    def wide(scale):
        return jnp.concatenate([scale] * (width // 128), axis=1)

    def select_and_cross(level, nodes):
        start = level * (level - 1) // 2
        tall = lines * level

        def one(n, _):
            above = row * 2 + n
            within, distance = [None] * level, [None] * level
            for up in range(level - 1, -1, -1):
                above = parents[up, above]
                within[up] = lax.rem(above, 2)
                distance[up] = lax.rem(row + rows_n - lax.div(above, 2), rows_n)

            def pick(refs, up, entry):
                value = None
                for k in range(level - up + 1):
                    ref = refs[(up, k)]
                    there = ref[within[up]] if entry is None else ref[within[up], entry]
                    value = there if value is None else lax.select(distance[up] == k, there, value)
                return value

            table = [pick(marks, up, None) for up in range(level)]
            for l in range(level):
                for m in range(level):
                    up = max(l, m)
                    if l == m:
                        entry, which = 2 * up, 2
                    elif l < m:
                        entry, which = l, 0
                    else:
                        entry, which = up + m, 1
                    code = pick(blocks, up, entry)
                    high, low = split(decode(code.astype(F32)) * wide(table[up][which]))
                    lhs[l * lines : (l + 1) * lines, m * width : (m + 1) * width] = high
                    lhs[tall + l * lines : tall + (l + 1) * lines, m * width : (m + 1) * width] = low
            both = jnp.dot(
                lhs[0 : 2 * tall, 0 : level * width],
                fulls[level - 1][pl.ds(n * level, level)].reshape(level * width, width),
                preferred_element_type=F32,
            )
            crossed = -(both[0:tall, :] + both[tall : 2 * tall, :])
            scale = scale_of(crossed)
            code = encode(crossed, scale)
            for l in range(level):
                cross_out[start + l, n] = crossed[l * lines : (l + 1) * lines, :]
                if level < LEVELS - 1:
                    blocks[(level, 0)][n, l] = code[l * lines : (l + 1) * lines, :].astype(BF16)
            if level < LEVELS - 1:
                marks[(level, 0)][n, 0] = jnp.broadcast_to(scale, (1, 128))
                pass_on(level, n, 0)
            turned = jnp.transpose(code, (1, 0)).astype(BF16)
            slab = 0 if joint(level) else n
            first = n * tall if joint(level) else 0
            for c in range(cols_n):
                piece = turned[c * lines : (c + 1) * lines, :]
                turn_out[level - 1][slab, c, :, first : first + min(tall, 128)] = piece[:, 0:128]
                if tall > 128:
                    turn_out[level - 1][2, c, :, n * lines : (n + 1) * lines] = piece[:, 128:tall]
            lane = lax.broadcasted_iota(jnp.int32, (1, 128), 1)
            mark = jnp.broadcast_to(scale, (1, 128))
            if joint(level) and n == 1:
                mark = jnp.where(lane < tall, mark_out[level - 1, 0], mark)
            mark_out[level - 1, slab] = mark
            if tall > 128:
                if n == 1:
                    mark = jnp.where(lane < lines, mark_out[level - 1, 2], mark)
                mark_out[level - 1, 2] = mark
                if n == 1:
                    send_turn(level, 2)
            if not joint(level):
                send_turn(level, n)
            return 0

        if joint(level):
            one(0, 0)
            one(1, 0)
            send_turn(level, 0)
        elif len(nodes) == 1:
            one(nodes[0], 0)
        else:
            lax.fori_loop(0, 2, one, 0)

    def send_turn(level, slab):
        def send(k, _):
            for copy in turn_copies(level, slab, k):
                copy.start()
            return 0

        lax.fori_loop(1, cols_n, send, 0)
        turn_in[level - 1][slab, col] = turn_out[level - 1][slab, col]
        mark_in[level - 1, slab, col] = mark_out[level - 1, slab]

    def open_turn(level, slab):
        for copy in turn_all(level, slab):
            copy.wait_recv()
        place = 128 if slabs_of(level) == 3 and slab == 2 else 0

        def undo(c, _):
            code = turn_in[level - 1][slab, c].astype(F32)
            opened[c, :, place : place + 128] = decode(code) * mark_in[level - 1, slab, c]
            return 0

        lax.fori_loop(0, cols_n, undo, 0)

    def finish_level(level):
        def one(n, _):
            if not joint(level):
                if slabs_of(level) == 3 and n == 0:
                    open_turn(level, 2)
                open_turn(level, n)
            for l in range(level):
                group = l + n * level if joint(level) else l if l < 4 else 4 + n
                for q in range(width // 128):
                    piece = None
                    for k in range(per):
                        source = opened[
                            q * per + k, :, (group // per) * 128 : (group // per) * 128 + 128
                        ]
                        shift = ((k - group % per) * lines) % 128
                        if shift:
                            source = pltpu.roll(source, shift, 1)
                        piece = source if piece is None else jnp.where(lane_of >= k * lines, source, piece)
                    high, low = split(piece)
                    lhs[0:lines, l * width + q * 128 : l * width + (q + 1) * 128] = high
                    lhs[lines : 2 * lines, l * width + q * 128 : l * width + (q + 1) * 128] = low
                    if level < LEVELS - 1:
                        turned_f32[l * lines : (l + 1) * lines, q * 128 : (q + 1) * 128] = piece
            if level < LEVELS - 1:
                whole = turned_f32[0 : level * lines, :]
                scale = scale_of(whole)
                code = encode(whole, scale).astype(BF16)
                for l in range(level):
                    blocks[(level, 0)][n, level + l] = code[l * lines : (l + 1) * lines, :]
                marks[(level, 0)][n, 1] = jnp.broadcast_to(scale, (1, 128))
                pass_on(level, n, 1)
            both = jnp.dot(
                lhs[0 : 2 * lines, 0 : level * width],
                fulls[level - 1][pl.ds(n * level, level)].reshape(level * width, width),
                preferred_element_type=F32,
            )
            marginal = base_of(level, n) - (both[0:lines, :] + both[lines : 2 * lines, :])
            marg_out[level, n] = marginal
            if level < LEVELS - 1:
                send_marginal(level, n, marginal)
            return 0

        if joint(level):
            open_turn(level, 0)
            one(0, 0)
            one(1, 0)
        elif slabs_of(level) == 2:
            lax.fori_loop(0, 2, one, 0)
        else:
            one(0, 0)
            one(1, 0)

    def keep_marginal(level, n, marginal):
        scale = scale_of(marginal)
        blocks[(level, 0)][n, 2 * level] = encode(marginal, scale).astype(BF16)
        for entry in range(3) if level == 0 else (2,):
            marks[(level, 0)][n, entry] = jnp.broadcast_to(scale, (1, 128))

    def send_marginal(level, n, marginal):
        keep_marginal(level, n, marginal)
        pass_on(level, n, 2)

    mask_factor(1)
    for n in range(2):
        marginal = base_of(0, n)
        marg_out[0, n] = marginal
        keep_marginal(0, n, marginal)
    for level in range(2, LEVELS):
        mask_factor(level)
    pl.semaphore_wait(barrier, 5)
    ring(1, 0)
    pass_on(0, 0, 2)
    pass_on(0, 1, 2)

    def run(jobs):
        for job in jobs:
            if job[0] == "pass":
                forward(*job[1:])
            else:
                ring(*job)

    run(PREPARE)
    for level in range(1, LEVELS):
        run(BEFORE[level])
        for up in range(level - 1, -1, -1):
            receive(up, level - up)
        run(FIRST[level])
        if level < LEVELS - 1:
            ring_end(level, 0)
            ring_end(level, 1)
            select_and_cross(level, (0, 1))
        else:
            ring_end(level, 0)
            select_and_cross(level, (0,))
            run(BETWEEN)
            ring_end(level, 1)
            select_and_cross(level, (1,))
        run(MIDDLE[level])
        finish_level(level)
        run(AFTER[level])

    for level in range(1, LEVELS):
        ring_sent(level)
        for slab in range(slabs_of(level)):
            for copy in turn_all(level, slab):
                copy.wait_send()
    for level, k in SENDS:
        for copy in hop(level, k):
            copy.wait_send()


def solution(mesh):
    rows_n, cols_n = mesh.shape["row"], mesh.shape["col"]

    def shards(panel, diag_inverse, parents, sizes):
        pairs, per, lines, width = panel.shape
        vmem = pl.BlockSpec(memory_space=pltpu.VMEM)
        smem = pl.BlockSpec(memory_space=pltpu.SMEM)
        dma = pltpu.SemaphoreType.DMA

        def turn_shape(level):
            return (slabs_of(level), cols_n, lines, 128)

        return pl.pallas_call(
            functools.partial(kernel, rows_n, cols_n),
            out_shape=(
                jax.ShapeDtypeStruct((pairs, per, lines, width), F32),
                jax.ShapeDtypeStruct((LEVELS, per, lines, width), F32),
            ),
            in_specs=[vmem, vmem, smem, smem],
            out_specs=(vmem, vmem),
            scratch_shapes=[
                *[pltpu.VMEM((2 * d, width, width), BF16) for d in range(1, 6)],
                *[pltpu.VMEM(turn_shape(d), BF16) for d in range(1, 6)],
                *[pltpu.VMEM(turn_shape(d), BF16) for d in range(1, 6)],
                *[pltpu.VMEM((per, 2 * level + 1, lines, width), BF16) for level, _ in HOPS],
                *[pltpu.VMEM((per, 3, 1, 128), F32) for _ in HOPS],
                pltpu.VMEM((320, 5 * width), BF16),
                pltpu.VMEM((cols_n, lines, 256), F32),
                pltpu.VMEM((4 * lines, width), F32),
                pltpu.VMEM((5, 3, 1, 128), F32),
                pltpu.VMEM((5, 3, cols_n, 1, 128), F32),
                dma((5,)),
                dma((5, 2, 4)),
                dma((5, 2)),
                dma((len(SENDS),)),
                dma((len(SENDS),)),
                dma((len(SENDS),)),
                dma((len(SENDS),)),
                dma((5, 3)),
                dma((5, 3)),
                dma((5, 3)),
                dma((5, 3)),
            ],
            compiler_params=pltpu.CompilerParams(
                collective_id=0, has_side_effects=True, vmem_limit_bytes=44000 * 1024
            ),
        )(panel, diag_inverse, parents, sizes)

    in_specs = (P(None, "row", "col", None), P(None, "row", "col", None), P(), P())
    out_specs = (P(None, "row", "col", None), P(None, "row", "col", None))
    return jax.shard_map(shards, mesh=mesh, in_specs=in_specs, out_specs=out_specs, check_vma=False)
```
